512 devices in a mesh: dp: 8 (over x, core), ctx: 64 (over y, z).
Axes of the slice: x: 4, y: 8, z: 8, core: 2. Of those that a mesh axis runs over, the one named last changes fastest.
Arguments:
- segment_tokens: bfloat16 [8, 16384, 1024], P('dp', 'ctx'), may hold values from -7 to 7
- upstream_grad: bfloat16 [8, 16384, 1024], P('dp', 'ctx'), may hold values from -16 to 16
- joint_weight: bfloat16 [1024, 3072], P('ctx', 'dp'), may hold values from -0.1875 to 0.1875
- output_weight: bfloat16 [1024, 1024], P('ctx', 'dp'), may hold values from -0.1875 to 0.1875
- norm_gain: bfloat16 [1024], replicated, may hold values from 0.5 to 1.5
- ancestors: int32 [8, 128, 5], P('dp', 'ctx'), may hold values from -1 to 126, as said below
- outline_depth: int32 [8, 128], P('dp'), may hold values from 0 to 5, as said below
Outputs:
- layer_output: bfloat16 [8, 16384, 1024], P('dp', 'ctx')
- input_gradient: bfloat16 [8, 16384, 1024], P('dp', 'ctx')
- weight_gradient: float32 [1024, 1024], P('dp', 'ctx')
- header_context: bfloat16 [8, 128, 1024], P('dp', 'ctx')
The draws below stay inside these ranges and needn't reach their ends.
Inputs may be any that keep to these rules, and one draw needn't show every extreme that they name: Entry l of segment i's list is the latest earlier segment j of level l with no segment of level l or less between j and i, for l below the depth of segment i; -1 where there is no such segment or l is not below that depth. Listed entries of one row increase. Some segment of every document lists 5 ancestors. `outline_depth`: segment i of every document has level i for i below 6; every later segment has level 1 or more; the last segment has level 5, and the one before it level 4 unless it is among the first 6.
All inputs are finite; a program needn't handle non-finite values.
Results may differ from the reference program's by a relative error of at most 0.012.
The reference program's roundings to bfloat16 on the way count: a program that leaves them out, or rounds other values in their place, can miss the bound.
Values may be sent and summed in bfloat16 or wider, within the bound.
A program may use at most 64 MiB of HBM per device.

```python
import jax
import jax.numpy as jnp
from jax import lax

D = 1024
H = 16
HD = 64
SEG = 128
LEVELS = 6
TOK_DEV = 256
DOCS = 8
DOC_LEN = 16384
DOC_SEGS = 128
N_CTX = 64


def draw_segment_tokens(key, part):
    first = jax.random.fold_in(key, 0)
    shape = (DOCS, DOC_LEN, D)
    values = jnp.clip(jax.random.normal(first, shape, jnp.float32), -6.0, 6.0)
    return values.astype(jnp.bfloat16)


def outline_levels(key):
    base = jax.random.fold_in(key, 11)
    first, second = jax.random.split(base)
    draw_one = jax.random.randint(first, (DOCS, DOC_SEGS), 0, LEVELS - 1, jnp.int32)
    draw_two = jax.random.randint(second, (DOCS, DOC_SEGS), 0, LEVELS - 1, jnp.int32)
    levels = LEVELS - 1 - jnp.minimum(draw_one, draw_two)
    index = jnp.arange(DOC_SEGS, dtype=jnp.int32)
    levels = jnp.where(index[None, :] == DOC_SEGS - 1, LEVELS - 1, levels)
    levels = jnp.where(index[None, :] == DOC_SEGS - 2, LEVELS - 2, levels)
    return jnp.where(index[None, :] < LEVELS, index[None, :], levels).astype(jnp.int32)


def outline_lists(levels):
    steps = jnp.arange(LEVELS, dtype=jnp.int32)

    def walk(latest, item):
        position, level = item
        listed = jnp.where(steps[None, :] < level[:, None], latest, -1)[:, :LEVELS - 1]
        latest = jnp.where(steps[None, :] == level[:, None], position, jnp.where(steps[None, :] > level[:, None], -1, latest))
        return (latest.astype(jnp.int32), listed.astype(jnp.int32))
    start = jnp.full((DOCS, LEVELS), -1, jnp.int32)
    _, lists = lax.scan(walk, start, (jnp.arange(DOC_SEGS, dtype=jnp.int32), levels.T))
    return jnp.transpose(lists, (1, 0, 2))


def draw_ancestors(key, part):
    return outline_lists(outline_levels(key))


def draw_outline_depth(key, part):
    return outline_levels(key)


def strengthened(drawn, stream_key, source, target, parts, factor):
    def block_of(axis_at):
        return (jnp.arange(drawn.shape[axis_at]) // (drawn.shape[axis_at] // parts)).reshape((-1,) + (1,) * (drawn.ndim - 1 - axis_at))

    first = jax.random.permutation(stream_key, parts)[block_of(target)]
    second = (block_of(target) + parts // 2) % parts
    return jnp.where((block_of(source) == first) | (block_of(source) == second), factor * drawn, drawn)


def steps_of(stream_key, dims, pieces, least, largest):
    factor_of = 1.0
    for axis_at, blocks in pieces:
        steps = jax.random.uniform(jax.random.fold_in(jax.random.fold_in(stream_key, 6), axis_at), (blocks,), jnp.float32, least / len(pieces), largest / len(pieces))
        factor_of = factor_of * jnp.repeat(jnp.exp(steps), dims[axis_at] // blocks).reshape((-1,) + (1,) * (len(dims) - 1 - axis_at))
    return factor_of


def normal_values(key, shape, scale, reach, cuts=(), held_as=jnp.bfloat16):
    entries = jax.random.normal(key, shape, jnp.float32) * scale
    if len(cuts) > 0:
        entries = steps_of(key, shape, cuts, -0.22, 0.18) * entries
    return jnp.clip(entries, min=-reach, max=reach).astype(held_as)


def noise_with(rng, dims, deviation, reach, shards, heavy, held_as=jnp.bfloat16):
    array = deviation * jax.random.normal(rng, dims, jnp.float32)
    if shards:
        array = array * steps_of(rng, dims, shards, -0.22, 0.18)
    return jnp.clip(strengthened(array, jax.random.fold_in(rng, 3), *heavy), -reach, reach).astype(held_as)


def setup_inputs(seed: int = 0) -> dict:
    key_list = jax.random.split(jax.random.key(seed), 8)
    segment_tokens = draw_segment_tokens(jax.random.fold_in(key_list[7], 71), 0)
    upstream_grad = noise_with(key_list[1], (DOCS, DOC_LEN, D), 1.0, 16.0, ((0, 8), (1, 64)), (1, 2, 64, 4.0))
    joint_weight = normal_values(key_list[2], (D, 3 * D), D ** -0.5, 0.1875, ((0, 64), (1, 8)))
    output_weight = normal_values(key_list[3], (D, D), D ** -0.5, 0.1875, ((0, 64), (1, 8)))
    norm_gain = jnp.clip(1.0 + 0.1 * jax.random.normal(key_list[4], (D,), jnp.float32), 0.5, 1.5).astype(jnp.bfloat16)
    ancestors = draw_ancestors(jax.random.fold_in(key_list[7], 71), 0)
    outline_depth = draw_outline_depth(jax.random.fold_in(key_list[7], 71), 0)
    return {"segment_tokens": segment_tokens, "upstream_grad": upstream_grad, "joint_weight": joint_weight, "output_weight": output_weight, "norm_gain": norm_gain, "ancestors": ancestors, "outline_depth": outline_depth}


def segment_block(inputs, upstream, joint_weight, output_weight, norm_gain):
    tokens_here = inputs.shape[0]
    segments_here = tokens_here // SEG
    scale = HD ** (-0.5)
    joint = jnp.dot(inputs, joint_weight, preferred_element_type=jnp.float32).astype(jnp.bfloat16)
    heads = joint.reshape(segments_here, SEG, 3, H, HD).astype(jnp.float32)
    queries = heads[:, :, 0]
    keys_all = heads[:, :, 1]
    values = heads[:, :, 2]
    scores = jnp.einsum('sqhe,skhe->shqk', queries, keys_all) * scale
    shares = jax.nn.softmax(scores, axis=-1)
    shares_low = lax.optimization_barrier(shares.astype(jnp.bfloat16)).astype(jnp.float32)
    mixed = jnp.einsum('shqk,skhe->sqhe', shares_low, values).reshape(tokens_here, D).astype(jnp.bfloat16)
    residual = inputs.astype(jnp.float32) + jnp.dot(mixed, output_weight, preferred_element_type=jnp.float32)
    average = lax.optimization_barrier(jnp.mean(residual, axis=-1, keepdims=True))
    centered = residual - average
    spread = lax.optimization_barrier(jnp.mean(centered * centered, axis=-1, keepdims=True))
    inverse = lax.rsqrt(spread + 1e-05)
    normed = centered * inverse
    gain_wide = norm_gain.astype(jnp.float32)
    layer_output = (normed * gain_wide).astype(jnp.bfloat16)
    scaled_grad = upstream.astype(jnp.float32) * gain_wide
    residual_grad = inverse * (scaled_grad - lax.optimization_barrier(jnp.mean(scaled_grad, axis=-1, keepdims=True)) - normed * lax.optimization_barrier(jnp.mean(scaled_grad * normed, axis=-1, keepdims=True)))
    residual_low = residual_grad.astype(jnp.bfloat16)
    partial_term = jnp.dot(mixed.T, residual_low, preferred_element_type=jnp.float32).astype(jnp.bfloat16)
    mixed_grad = jnp.dot(residual_low, output_weight.T, preferred_element_type=jnp.float32).astype(jnp.bfloat16)
    mixed_grad = mixed_grad.reshape(segments_here, SEG, H, HD).astype(jnp.float32)
    shares_grad = jnp.einsum('sqhe,skhe->shqk', mixed_grad, values)
    scores_grad = shares * (shares_grad - lax.optimization_barrier(jnp.sum(shares_grad * shares, axis=-1, keepdims=True))) * scale
    scores_grad = lax.optimization_barrier(scores_grad.astype(jnp.bfloat16)).astype(jnp.float32)
    query_grad = jnp.einsum('shqk,skhe->sqhe', scores_grad, keys_all)
    key_grad = jnp.einsum('shqk,sqhe->skhe', scores_grad, queries)
    value_grad = jnp.einsum('shqk,sqhe->skhe', shares_low, mixed_grad)
    joint_grad = jnp.stack([query_grad, key_grad, value_grad], axis=2).reshape(tokens_here, 3 * D).astype(jnp.bfloat16)
    input_gradient = (residual_grad + jnp.dot(joint_grad, joint_weight.T, preferred_element_type=jnp.float32)).astype(jnp.bfloat16)
    header_rows = joint.reshape(segments_here, SEG, 3 * D)[:, 0, :]
    return (layer_output, input_gradient, partial_term, header_rows)

def header_section(header_rows, ancestors, outline_depth):
    scale = HD ** (-0.5)
    heads = header_rows.reshape(DOCS, DOC_SEGS, 3, H, HD).astype(jnp.float32)
    scores = jnp.einsum('dihe,djhe->dhij', heads[:, :, 0], heads[:, :, 1]) * scale
    slopes = 2.0 ** (-(jnp.arange(H, dtype=jnp.float32) + 1.0) * 4.0 / H)
    levels = outline_depth.astype(jnp.float32)
    bias = -slopes[None, :, None, None] * (levels[:, None, :, None] - levels[:, None, None, :])
    positions = jnp.arange(DOC_SEGS, dtype=jnp.int32)
    listed = jnp.any(ancestors[:, :, :, None] == positions[None, None, None, :], axis=2)
    kept = listed | (positions[:, None] == positions[None, :])[None]
    masked = jnp.where(kept[:, None], scores + bias, -1e+30)
    shares = jax.nn.softmax(masked, axis=-1)
    shares_low = lax.optimization_barrier(shares.astype(jnp.bfloat16)).astype(jnp.float32)
    context = jnp.einsum('dhij,djhe->dihe', shares_low, heads[:, :, 2])
    return context.reshape(DOCS, DOC_SEGS, D).astype(jnp.bfloat16)

def reference(segment_tokens, upstream_grad, joint_weight, output_weight, norm_gain, ancestors, outline_depth):
    blocks = DOCS * N_CTX
    token_blocks = segment_tokens.reshape(blocks, TOK_DEV, D)
    grad_blocks = upstream_grad.reshape(blocks, TOK_DEV, D)

    def advance(total, pair):
        layer_out, input_grad, partial_term, header_rows = segment_block(pair[0], pair[1], joint_weight, output_weight, norm_gain)
        return (total + partial_term.astype(jnp.float32), (layer_out, input_grad, header_rows))
    weight_gradient, (outputs, gradients, headers) = lax.scan(advance, jnp.zeros((D, D), jnp.float32), (token_blocks, grad_blocks))
    layer_output = outputs.reshape(DOCS, DOC_LEN, D)
    input_gradient = gradients.reshape(DOCS, DOC_LEN, D)
    header_context = header_section(headers.reshape(DOCS, DOC_SEGS, 3 * D), ancestors, outline_depth)
    return (layer_output, input_gradient, weight_gradient, header_context)
```

```python
import functools

import jax
import jax.numpy as jnp
from jax import lax
from jax.experimental import pallas as pl
from jax.experimental.pallas import tpu as pltpu
from jax.sharding import PartitionSpec as P

HD = 64
SEG = 128
BF = jnp.bfloat16
F32 = jnp.float32
MESH = pl.DeviceIdType.MESH
TORUS = (4, 8, 8)
NT = (((1,), (1,)), ((), ()))


def far_first(n):
    return sorted(range(1, n), key=lambda t: -min(t, n - t))


def layer_kernel(
    dims,
    x_ref,
    u_ref,
    wj_ref,
    wo_ref,
    gain_ref,
    out_ref,
    grad_ref,
    dw_ref,
    panel_ref,
    hq_ref,
    gj,
    go,
    joint,
    shares_buf,
    mixed,
    res,
    rlow,
    rlow_t,
    part,
    r0,
    a1,
    r1,
    a2,
    r2,
    a3,
    r3,
    mgrad,
    jgrad,
    hfl,
    hsend,
    ring_send,
    ring_recv,
    sems,
):
    X, Y, Z = dims
    D = x_ref.shape[1]
    pairs = D // 128
    rows = wj_ref.shape[0]
    wide = wj_ref.shape[1]
    scale = HD ** (-0.5)
    dp = lax.axis_index("dp")
    ctx = lax.axis_index("ctx")
    x, core = dp // 2, dp % 2
    y, z = ctx // Z, ctx % Z
    every = slice(None)

    def on_core(body):
        for c in (0, 1):

            @pl.when(core == c)
            def _():
                body(c)

    def send(src, dst, ssem, rsem, peer):
        pltpu.make_async_remote_copy(
            src_ref=src, dst_ref=dst, send_sem=ssem, recv_sem=rsem, device_id=peer, device_id_type=MESH
        ).start()

    def settle(ref, sem):
        pltpu.make_async_copy(ref, ref, sem).wait()

    def first_axis(c):
        return (Y, y) if c == 0 else (Z, z)

    def second_axis(c):
        return (Z, z) if c == 0 else (Y, y)

    def at_first(c, f):
        return (dp, f * Z + z) if c == 0 else (dp, y * Z + f)

    def at_second(c, s):
        return (dp, y * Z + s) if c == 0 else (dp, s * Z + z)

    def yz(c, f, s):
        return (f, s) if c == 0 else (s, f)

    def at_x(c, k):
        return (k * 2 + c, ctx)

    partner = (x * 2 + 1 - core, ctx)

    barrier = pltpu.get_barrier_semaphore()
    for t in range(1, X):
        pl.semaphore_signal(barrier, device_id=(((x + t) % X) * 2 + core, ctx), device_id_type=MESH)
    for t in range(1, Y):
        pl.semaphore_signal(barrier, device_id=(dp, ((y + t) % Y) * Z + z), device_id_type=MESH)
    for t in range(1, Z):
        pl.semaphore_signal(barrier, device_id=(dp, y * Z + (z + t) % Z), device_id_type=MESH)
    pl.semaphore_signal(barrier, device_id=partner, device_id_type=MESH)
    pl.semaphore_wait(barrier, X + Y + Z - 2)

    def gather_start(c):
        own = pltpu.make_async_copy(wj_ref, gj.at[x, c, y, z], sems.at[0])
        own_out = pltpu.make_async_copy(wo_ref, go.at[x, c, y, z], sems.at[1])
        own.start()
        own_out.start()
        for t in range(1, X):
            send(wj_ref, gj.at[x, c, y, z], sems.at[2], sems.at[3], at_x(c, (x + t) % X))
        n, f = first_axis(c)
        for t in far_first(n):
            send(wo_ref, go.at[x, c, y, z], sems.at[4], sems.at[5], at_first(c, (f + t) % n))
        own.wait()
        own_out.wait()
        if X > 1:
            settle(gj.at[pl.ds(0, X - 1), c, y, z], sems.at[3])
        for t in far_first(n):
            send(gj.at[:, c, y, z], gj.at[:, c, y, z], sems.at[6], sems.at[7], at_first(c, (f + t) % n))
        m, s = second_axis(c)
        settle(go.at[(x, c) + yz(c, pl.ds(0, n - 1), s)], sems.at[5])
        for t in far_first(m):
            ref = go.at[(x, c) + yz(c, every, s)]
            send(ref, ref, sems.at[8], sems.at[9], at_second(c, (s + t) % m))
        settle(gj.at[(every, c) + yz(c, pl.ds(0, n - 1), s)], sems.at[7])

    def carried(sign, k, j, m):
        if 2 * k < m:
            return True
        return 2 * k == m and (j < (X + 1) // 2) == (sign == 0)

    def ring(c):
        m, s = second_axis(c)

        def chunk(j, source):
            return gj.at[(j, c) + yz(c, every, source)]

        def push(sign, k, j):
            step = 1 if sign == 0 else m - 1
            ref = chunk(j, (s + (k - 1) * (m - step)) % m)
            return pltpu.make_async_remote_copy(
                src_ref=ref,
                dst_ref=ref,
                send_sem=ring_send.at[sign, k - 1, j],
                recv_sem=ring_recv.at[sign, k - 1, j],
                device_id=at_second(c, (s + step) % m),
                device_id_type=MESH,
            )

        for j in range(X):
            for sign in (0, 1):
                if carried(sign, 1, j, m):
                    push(sign, 1, j).start()
        ref = gj.at[(every, c) + yz(c, every, s)]
        send(ref, ref, sems.at[10], sems.at[11], partner)
        for k in range(1, m // 2 + 1):
            for j in range(X):
                for sign in (0, 1):
                    if not carried(sign, k, j, m):
                        continue
                    back = (m - 1) if sign == 0 else 1
                    ref = chunk(j, (s + k * back) % m)
                    settle(ref, ring_recv.at[sign, k - 1, j])
                    if carried(sign, k + 1, j, m):
                        push(sign, k + 1, j).start()
                    send(ref, ref, sems.at[10], sems.at[11], partner)
            if k == 1:
                settle(go.at[(x, c) + yz(c, every, pl.ds(0, m - 1))], sems.at[9])
                for t in range(1, X):
                    send(go.at[x, c], go.at[x, c], sems.at[12], sems.at[13], at_x(c, (x + t) % X))
        settle(gj.at[:, 1 - c], sems.at[11])

    on_core(gather_start)
    on_core(ring)

    lane = lax.broadcasted_iota(jnp.int32, (SEG, 128), 1)
    low_half = lane < HD

    def apart(pair):
        nothing = jnp.zeros_like(pair)
        return jnp.concatenate(
            [jnp.where(low_half, pair, nothing), jnp.where(low_half, nothing, pair)], axis=0
        )

    def joined(both):
        return jnp.where(low_half, both[:SEG], both[SEG:])

    def project(j, carry):
        weights = jnp.concatenate(
            [gj[j, 0].reshape(D, wide), gj[j, 1].reshape(D, wide)], axis=1
        )
        product = jnp.dot(x_ref[...], weights, preferred_element_type=F32).astype(BF)
        per = 2 * wide // 128
        for i in range(per):
            joint[per * j + i] = product[:, 128 * i : 128 * (i + 1)]
        return carry

    lax.fori_loop(0, X, project, 0)

    def hand_output_weights(c):
        if X > 1:
            settle(go.at[pl.ds(0, X - 1), c], sems.at[13])
        send(go.at[:, c], go.at[:, c], sems.at[14], sems.at[15], partner)

    on_core(hand_output_weights)

    for s in range(2):
        for g in range(pairs):
            hq_ref[s, g : g + 1, :] = joint[g, SEG * s : SEG * s + 16, :].astype(F32)[0:1]
        for g in range(2 * pairs):
            hfl[s, g : g + 1, :] = joint[pairs + g, SEG * s : SEG * s + 16, :].astype(F32)[0:1]
    hsend[...] = hfl[...].astype(BF)

    def attend(it, carry):
        p, s = it // 2, it % 2
        span = pl.ds(pl.multiple_of(s * SEG, SEG), SEG)
        queries = apart(joint[p, span, :])
        scores = lax.dot_general(queries, joint[pairs + p, span, :], NT, preferred_element_type=F32) * scale
        raised = jnp.exp(scores - jnp.max(scores, axis=-1, keepdims=True))
        shares = raised * (1.0 / jnp.sum(raised, axis=-1, keepdims=True))
        shares_buf[it] = shares
        both = jnp.dot(shares.astype(BF), joint[2 * pairs + p, span, :], preferred_element_type=F32)
        mixed[p, span, :] = joined(both).astype(BF)
        return carry

    lax.fori_loop(0, 2 * pairs, attend, 0)

    def headers_first(c):
        own = pltpu.make_async_copy(hsend, panel_ref.at[y, z], sems.at[0])
        own.start()
        n, f = first_axis(c)
        for t in far_first(n):
            send(hsend, panel_ref.at[y, z], sems.at[16], sems.at[17], at_first(c, (f + t) % n))
        own.wait()

    on_core(headers_first)

    settle_out = lambda c: settle(go.at[:, 1 - c], sems.at[15])
    on_core(settle_out)

    def mixed_all():
        return jnp.concatenate([mixed[p] for p in range(pairs)], axis=1)

    def project_out(j, carry):
        weights = jnp.concatenate([go[j, 0].reshape(D, 128), go[j, 1].reshape(D, 128)], axis=1)
        product = jnp.dot(mixed_all(), weights, preferred_element_type=F32)
        res[:, pl.ds(pl.multiple_of(j * 256, 256), 256)] = product
        return carry

    lax.fori_loop(0, X, project_out, 0)

    def headers_second(c):
        n, f = first_axis(c)
        m, s = second_axis(c)
        settle(panel_ref.at[yz(c, pl.ds(0, n - 1), s)], sems.at[17])
        for t in far_first(m):
            ref = panel_ref.at[yz(c, every, s)]
            send(ref, ref, sems.at[18], sems.at[19], at_second(c, (s + t) % m))

    on_core(headers_second)

    block = 32

    def norm(i, carry):
        span = pl.ds(pl.multiple_of(i * block, block), block)
        gain = gain_ref[...].astype(F32)
        residual = x_ref[span, :].astype(F32) + res[span, :]
        average = jnp.mean(residual, axis=-1, keepdims=True)
        centered = residual - average
        spread = jnp.mean(centered * centered, axis=-1, keepdims=True)
        inverse = lax.rsqrt(spread + 1e-05)
        normed = centered * inverse
        out_ref[span, :] = (normed * gain).astype(BF)
        scaled = u_ref[span, :].astype(F32) * gain
        first = jnp.mean(scaled, axis=-1, keepdims=True)
        second = jnp.mean(scaled * normed, axis=-1, keepdims=True)
        gradient = inverse * (scaled - first - normed * second)
        res[span, :] = gradient
        rlow[span, :] = gradient.astype(BF)
        return carry

    lax.fori_loop(0, 2 * SEG // block, norm, 0)

    for i in range(pairs):
        rlow_t[128 * i : 128 * (i + 1), :] = rlow[:, 128 * i : 128 * (i + 1)].T

    def partial_of(j, carry):
        both = jnp.concatenate([mixed[2 * j], mixed[2 * j + 1]], axis=1)
        product = jnp.dot(rlow_t[...], both, preferred_element_type=F32).astype(BF)
        part[j, 0] = product[:, :128].reshape(Y, Z, rows, 128)
        part[j, 1] = product[:, 128:].reshape(Y, Z, rows, 128)
        return carry

    lax.fori_loop(0, X, partial_of, 0)

    on_core(lambda c: send(part.at[:, 1 - c], r0, sems.at[20], sems.at[21], partner))

    tall = 2 if Y % 2 == 0 and Z * rows == 128 else 1
    height = tall * Z * rows

    def rows_of(ref, i, width):
        start = i * tall
        return jnp.concatenate(
            [
                ref[j, c, pl.ds(start, tall)].reshape(height, width)
                for j in range(X)
                for c in (0, 1)
            ],
            axis=1,
        )

    def mix_back(i, carry):
        product = lax.dot_general(rlow[...], rows_of(go, i, 128), NT, preferred_element_type=F32).astype(BF)
        for k in range(height // 128):
            mgrad[(height // 128) * i + k] = product[:, 128 * k : 128 * (k + 1)]
        return carry

    lax.fori_loop(0, Y // tall, mix_back, 0)

    settle(r0, sems.at[21])

    def pair_sum(i, carry):
        j, k = i // Y, i % Y
        a1[j, k] = (part[j, core, k].astype(F32) + r0[j, k].astype(F32)).astype(BF)
        return carry

    lax.fori_loop(0, X * Y, pair_sum, 0)

    def reduce_first(c):
        n, f = first_axis(c)
        own = pltpu.make_async_copy(a1.at[(every,) + yz(c, f, every)], r1.at[f], sems.at[0])
        own.start()
        for t in far_first(n):
            g = (f + t) % n
            send(a1.at[(every,) + yz(c, g, every)], r1.at[f], sems.at[22], sems.at[23], at_first(c, g))
        own.wait()

    on_core(reduce_first)

    def attend_back(it, carry):
        p, s = it // 2, it % 2
        span = pl.ds(pl.multiple_of(s * SEG, SEG), SEG)
        keys, values = joint[pairs + p, span, :], joint[2 * pairs + p, span, :]
        outer = apart(mgrad[p, span, :])
        shares = shares_buf[it]
        shares_grad = lax.dot_general(outer, values, NT, preferred_element_type=F32)
        inner = jnp.sum(shares_grad * shares, axis=-1, keepdims=True)
        scores_grad = (shares * (shares_grad - inner) * scale).astype(BF)
        query_grad = jnp.dot(scores_grad, keys, preferred_element_type=F32)
        jgrad[p, span, :] = joined(query_grad).astype(BF)
        key_grad = jnp.dot(scores_grad.T, apart(joint[p, span, :]), preferred_element_type=F32)
        jgrad[pairs + p, span, :] = key_grad.astype(BF)
        value_grad = jnp.dot(shares.astype(BF).T, outer, preferred_element_type=F32)
        jgrad[2 * pairs + p, span, :] = value_grad.astype(BF)
        return carry

    lax.fori_loop(0, 2 * pairs, attend_back, 0)

    def input_back(i, carry):
        left = jnp.concatenate([jgrad[g] for g in range(3 * pairs)], axis=1)
        product = lax.dot_general(left, rows_of(gj, i, wide), NT, preferred_element_type=F32)
        span = pl.ds(pl.multiple_of(i * height, height), height)
        grad_ref[:, span] = (res[:, span] + product).astype(BF)
        return carry

    lax.fori_loop(0, Y // tall, input_back, 0)

    settle(r1.at[pl.ds(0, Y - 1)], sems.at[23])

    def first_sum(i, carry):
        j = i
        total = r1[0, j].astype(F32)
        for k in range(1, Y):
            total = total + r1[k, j].astype(F32)
        a2[j] = total
        return carry

    lax.fori_loop(0, X, first_sum, 0)

    def reduce_second(c):
        m, s = second_axis(c)
        own = pltpu.make_async_copy(a2.at[:, s], r2.at[s], sems.at[0])
        own.start()
        for t in far_first(m):
            g = (s + t) % m
            send(a2.at[:, g], r2.at[s], sems.at[24], sems.at[25], at_second(c, g))
        own.wait()

    on_core(reduce_second)
    settle(r2.at[pl.ds(0, Y - 1)], sems.at[25])
    total = r2[0]
    for k in range(1, Y):
        total = total + r2[k]
    a3[...] = total

    own = pltpu.make_async_copy(a3.at[x], r3.at[x], sems.at[0])
    own.start()
    for t in range(1, X):
        k = (x + t) % X
        send(a3.at[k], r3.at[x], sems.at[26], sems.at[27], (k * 2 + core, ctx))
    own.wait()
    if X > 1:
        settle(r3.at[pl.ds(0, X - 1)], sems.at[27])
    final = r3[0]
    for k in range(1, X):
        final = final + r3[k]
    dw_ref[...] = final

    def drain(c):
        n, f = first_axis(c)
        m, s = second_axis(c)
        if X > 1:
            settle(gj.at[pl.ds(0, X - 1), c, y, z], sems.at[2])
            settle(go.at[pl.ds(0, X - 1), c], sems.at[12])
            settle(r3.at[pl.ds(0, X - 1)], sems.at[26])
        settle(go.at[(x, c) + yz(c, pl.ds(0, n - 1), s)], sems.at[4])
        settle(gj.at[(every, c) + yz(c, pl.ds(0, n - 1), s)], sems.at[6])
        settle(go.at[(x, c) + yz(c, every, pl.ds(0, m - 1))], sems.at[8])
        settle(gj.at[:, c], sems.at[10])
        settle(go.at[:, c], sems.at[14])
        settle(panel_ref.at[yz(c, pl.ds(0, n - 1), s)], sems.at[16])
        settle(panel_ref.at[yz(c, every, pl.ds(0, m - 1))], sems.at[18])
        settle(panel_ref.at[yz(c, every, pl.ds(0, m - 1))], sems.at[19])
        settle(r0, sems.at[20])
        settle(r1.at[pl.ds(0, n - 1)], sems.at[22])
        settle(r2.at[pl.ds(0, m - 1)], sems.at[24])
        for k in range(1, m // 2 + 1):
            for j in range(X):
                for sign in (0, 1):
                    if carried(sign, k, j, m):
                        settle(gj.at[(j, c) + yz(c, every, s)], ring_send.at[sign, k - 1, j])

    on_core(drain)


def call_layer(dims, tokens, upstream, joint_weight, output_weight, gain):
    X, Y, Z = dims
    T, D = tokens.shape
    pairs = D // 128
    rows, wide = joint_weight.shape
    vmem = pl.BlockSpec(memory_space=pltpu.VMEM)
    V = pltpu.VMEM
    return pl.pallas_call(
        functools.partial(layer_kernel, dims),
        out_shape=(
            jax.ShapeDtypeStruct((T, D), BF),
            jax.ShapeDtypeStruct((T, D), BF),
            jax.ShapeDtypeStruct((rows, 128), F32),
            jax.ShapeDtypeStruct((Y, Z, 2, 2 * pairs, 128), BF),
            jax.ShapeDtypeStruct((2, pairs, 128), F32),
        ),
        in_specs=[vmem] * 5,
        out_specs=(vmem,) * 5,
        scratch_shapes=[
            V((X, 2, Y, Z, rows, wide), BF),
            V((X, 2, Y, Z, rows, 128), BF),
            V((3 * pairs, T, 128), BF),
            V((2 * pairs, 2 * SEG, SEG), F32),
            V((pairs, T, 128), BF),
            V((T, D), F32),
            V((T, D), BF),
            V((D, T), BF),
            V((X, 2, Y, Z, rows, 128), BF),
            V((X, Y, Z, rows, 128), BF),
            V((X, Y, Z, rows, 128), BF),
            V((Y, X, Z, rows, 128), BF),
            V((X, Z, rows, 128), F32),
            V((Y, X, rows, 128), F32),
            V((X, rows, 128), F32),
            V((X, rows, 128), F32),
            V((pairs, T, 128), BF),
            V((3 * pairs, T, 128), BF),
            V((2, 2 * pairs, 128), F32),
            V((2, 2 * pairs, 128), BF),
            pltpu.SemaphoreType.DMA((2, max(Y // 2, 1), X)),
            pltpu.SemaphoreType.DMA((2, max(Y // 2, 1), X)),
            pltpu.SemaphoreType.DMA((28,)),
        ],
        compiler_params=pltpu.CompilerParams(collective_id=0, has_side_effects=True),
        name="segment_layer",
    )(tokens, upstream, joint_weight, output_weight, gain)


def on_device(
    dims, segment_tokens, upstream_grad, joint_weight, output_weight, norm_gain, ancestors, outline_depth
):
    T, D = segment_tokens.shape[1:]
    H = D // HD
    scale = HD ** (-0.5)
    here = T // SEG
    layer_output, input_gradient, share_t, panel, header_queries = call_layer(
        dims, segment_tokens[0], upstream_grad[0], joint_weight, output_weight, norm_gain.reshape(1, D)
    )
    weight_gradient = share_t.T
    total_segments = dims[1] * dims[2] * here
    panel_heads = panel.reshape(total_segments, 2, H, HD)
    header_queries = header_queries.reshape(here, H, HD).astype(BF)
    header_scores = (
        jnp.einsum("ihe,jhe->hij", header_queries, panel_heads[:, 0], preferred_element_type=F32) * scale
    )
    first_segment = lax.axis_index("ctx") * here
    all_levels = outline_depth[0].astype(F32)
    own_levels = lax.dynamic_slice_in_dim(all_levels, first_segment, here)
    slopes = 2.0 ** (-(jnp.arange(H, dtype=F32) + 1.0) * 4.0 / H)
    bias = -slopes[:, None, None] * (own_levels[None, :, None] - all_levels[None, None, :])
    positions = jnp.arange(total_segments, dtype=jnp.int32)
    own_positions = first_segment + jnp.arange(here, dtype=jnp.int32)
    listed = jnp.any(ancestors[0][:, :, None] == positions[None, None, :], axis=1)
    kept = listed | (own_positions[:, None] == positions[None, :])
    masked = jnp.where(kept[None], header_scores + bias, -1e30)
    header_top = jnp.max(masked, axis=-1, keepdims=True)
    header_raised = jnp.exp(masked - header_top)
    header_shares = (header_raised / jnp.sum(header_raised, axis=-1, keepdims=True)).astype(BF)
    context = jnp.einsum("hij,jhe->ihe", header_shares, panel_heads[:, 1], preferred_element_type=F32)
    header_context = context.reshape(here, D).astype(BF)
    return (layer_output[None], input_gradient[None], weight_gradient, header_context[None])


def solution(mesh, dims=TORUS):
    return jax.shard_map(
        functools.partial(on_device, dims),
        mesh=mesh,
        in_specs=(
            P("dp", "ctx", None),
            P("dp", "ctx", None),
            P("ctx", "dp"),
            P("ctx", "dp"),
            P(),
            P("dp", "ctx", None),
            P("dp", None),
        ),
        out_specs=(
            P("dp", "ctx", None),
            P("dp", "ctx", None),
            P("dp", "ctx"),
            P("dp", "ctx", None),
        ),
        check_vma=False,
    )
```

```python
import functools

import jax
import jax.numpy as jnp
from jax import lax
from jax.experimental import pallas as pl
from jax.experimental.pallas import tpu as pltpu
from jax.sharding import PartitionSpec as P

HD = 64
SEG = 128
BF = jnp.bfloat16
F32 = jnp.float32
MESH = pl.DeviceIdType.MESH
TORUS = (4, 8, 8)
NT = (((1,), (1,)), ((), ()))


def far_first(n):
    return sorted(range(1, n), key=lambda t: -min(t, n - t))


def layer_kernel(
    dims,
    tokens_ref,
    upstream_ref,
    wj_ref,
    wo_ref,
    gain_hbm,
    lists_hbm,
    depth_hbm,
    out_hbm,
    grad_hbm,
    dw_ref,
    context_ref,
    x_ref,
    u_ref,
    out_ref,
    grad_ref,
    panel,
    gj,
    go,
    joint,
    shares_buf,
    mixed,
    res,
    rlow,
    rlow_t,
    part,
    r0,
    a1,
    r1,
    tie_in,
    tie_sum,
    tie_got,
    a2,
    a2_low,
    r2,
    a3,
    r3,
    mgrad,
    jgrad,
    hq,
    hfl,
    hsend,
    wide_context,
    first_recv,
    ring_recv,
    out_recv,
    line_recv,
    gain_ref,
    lists_ref,
    depth_ref,
    sems,
):
    X, Y, Z = dims
    D = x_ref.shape[1]
    pairs = D // 128
    rows = wj_ref.shape[0]
    wide = wj_ref.shape[1]
    scale = HD ** (-0.5)
    dp = lax.axis_index("dp")
    ctx = lax.axis_index("ctx")
    x, core = dp // 2, dp % 2
    y, z = ctx // Z, ctx % Z
    every = slice(None)

    def on_core(body):
        for c in (0, 1):

            @pl.when(core == c)
            def _():
                body(c)

    def send(src, dst, ssem, rsem, peer):
        pltpu.make_async_remote_copy(
            src_ref=src, dst_ref=dst, send_sem=ssem, recv_sem=rsem, device_id=peer, device_id_type=MESH
        ).start()

    def settle(ref, sem):
        pltpu.make_async_copy(ref, ref, sem).wait()

    def first_axis(c):
        return (Y, y) if c == 0 else (Z, z)

    def second_axis(c):
        return (Z, z) if c == 0 else (Y, y)

    def at_first(c, f):
        return (dp, f * Z + z) if c == 0 else (dp, y * Z + f)

    def at_second(c, s):
        return (dp, y * Z + s) if c == 0 else (dp, s * Z + z)

    def yz(c, f, s):
        return (f, s) if c == 0 else (s, f)

    def at_x(c, k):
        return (k * 2 + c, ctx)

    partner = (x * 2 + 1 - core, ctx)

    tokens_in = pltpu.make_async_copy(tokens_ref, x_ref, sems.at[28])
    upstream_in = pltpu.make_async_copy(upstream_ref, u_ref, sems.at[29])
    tokens_in.start()
    upstream_in.start()
    small = [
        pltpu.make_async_copy(gain_hbm, gain_ref, sems.at[36]),
        pltpu.make_async_copy(lists_hbm, lists_ref, sems.at[37]),
        pltpu.make_async_copy(depth_hbm, depth_ref, sems.at[38]),
    ]
    for copy in small:
        copy.start()

    barrier = pltpu.get_barrier_semaphore()
    for t in range(1, X):
        pl.semaphore_signal(barrier, device_id=(((x + t) % X) * 2 + core, ctx), device_id_type=MESH)
    for t in range(1, Y):
        pl.semaphore_signal(barrier, device_id=(dp, ((y + t) % Y) * Z + z), device_id_type=MESH)
    for t in range(1, Z):
        pl.semaphore_signal(barrier, device_id=(dp, y * Z + (z + t) % Z), device_id_type=MESH)
    pl.semaphore_signal(barrier, device_id=partner, device_id_type=MESH)
    pl.semaphore_wait(barrier, X + Y + Z - 2)

    def gather(c):
        n, f = first_axis(c)
        m, s = second_axis(c)

        def block(o, q):
            return gj.at[(every, c) + yz(c, (f + o) % n, (s + q) % m)]

        def out_block(q):
            return go.at[(x, c) + yz(c, every, (s + q) % m)]

        def hop(ref, ssem, rsem, peer):
            send(ref, ref, ssem, rsem, peer)

        def step(sign):
            return 1 if sign == 0 else -1

        def on_second(sign, k, o):
            return 2 * k < m or (2 * k == m and (2 * o < n) == (sign == 0))

        def on_out(sign, k):
            return 2 * k < m or (2 * k == m and sign == 1)

        def push_second(sign, k, o):
            if on_second(sign, k, o):
                hop(
                    block(o, -step(sign) * (k - 1) % m),
                    sems.at[7],
                    ring_recv.at[sign, k - 1, o],
                    at_second(c, (s + step(sign) % m) % m),
                )

        def push_out(sign, k):
            if on_out(sign, k):
                hop(
                    out_block(-step(sign) * (k - 1) % m),
                    sems.at[8],
                    out_recv.at[sign, k - 1],
                    at_second(c, (s + step(sign) % m) % m),
                )

        def share(ref):
            hop(ref, sems.at[10], sems.at[11], partner)

        own = pltpu.make_async_copy(wj_ref, gj.at[x, c, y, z], sems.at[0])
        own_out = pltpu.make_async_copy(wo_ref, go.at[x, c, y, z], sems.at[1])
        own.start()
        own_out.start()
        for t in range(1, X):
            send(wj_ref, gj.at[x, c, y, z], sems.at[2], sems.at[3], at_x(c, (x + t) % X))
        near = sorted(range(1, n), key=lambda t: min(t, n - t))
        for t in near:
            send(wo_ref, go.at[x, c, y, z], sems.at[4], sems.at[5], at_first(c, (f + t) % n))
        own.wait()
        own_out.wait()
        if X > 1:
            settle(gj.at[pl.ds(0, X - 1), c, y, z], sems.at[3])
        for t in near:
            hop(block(0, 0), sems.at[6], first_recv.at[t], at_first(c, (f + t) % n))
        for sign in (0, 1):
            push_second(sign, 1, 0)
        share(block(0, 0))

        arrival = {-t % n: 1.5 + i for i, t in enumerate(near)}
        arrival[0] = 0.0
        events = [(arrival[o], 0, 0, "first", 0, o) for o in range(1, n)]
        for sign in (0, 1):
            for k in range(1, m // 2 + 1):
                for o in range(n):
                    if on_second(sign, k, o):
                        events.append((arrival[o] + 2.9 * k, 2, sign, "second", k, o))
                if on_out(sign, k):
                    events.append((3 + 2.9 * k, 1, sign, "out", k, 0))
        events.append((3, 1, 0, "plane", 0, 0))
        events.sort(key=lambda e: (e[0], e[1], -e[4], e[2]))
        left = sum(e[3] == "out" for e in events)
        for _, _, sign, kind, k, o in events:
            if kind == "first":
                settle(block(o, 0), first_recv.at[-o % n])
                for way in (0, 1):
                    push_second(way, 1, o)
                share(block(o, 0))
            elif kind == "second":
                ref = block(o, -step(sign) * k % m)
                settle(ref, ring_recv.at[sign, k - 1, o])
                push_second(sign, k + 1, o)
                share(ref)
            elif kind == "plane":
                settle(go.at[(x, c) + yz(c, pl.ds(0, n - 1), s)], sems.at[5])
                for way in (0, 1):
                    push_out(way, 1)
            else:
                settle(out_block(-step(sign) * k % m), out_recv.at[sign, k - 1])
                push_out(sign, k + 1)
                left -= 1
                if left == 0:
                    for sign in range(min(X - 1, 2)):
                        hop(go.at[x, c], sems.at[12], line_recv.at[0, sign], at_x(c, (x + step(sign)) % X))
        for sign in range(min(X - 1, 2)):
            settle(go.at[x, c], line_recv.at[0, sign])
            if X == 4:
                ref = go.at[(x - step(sign)) % X, c, pl.ds(sign * Y // 2, Y // 2)]
                hop(ref, sems.at[13], line_recv.at[1, sign], at_x(c, (x + step(sign)) % X))
        settle(gj.at[:, 1 - c], sems.at[11])

    on_core(gather)
    tokens_in.wait()

    lane = lax.broadcasted_iota(jnp.int32, (SEG, 128), 1)
    low_half = lane < HD

    def apart(pair):
        nothing = jnp.zeros_like(pair)
        return jnp.concatenate(
            [jnp.where(low_half, pair, nothing), jnp.where(low_half, nothing, pair)], axis=0
        )

    def joined(both):
        return jnp.where(low_half, both[:SEG], both[SEG:])

    def project(j, carry):
        weights = jnp.concatenate(
            [gj[j, 0].reshape(D, wide), gj[j, 1].reshape(D, wide)], axis=1
        )
        product = jnp.dot(x_ref[...], weights, preferred_element_type=F32).astype(BF)
        per = 2 * wide // 128
        for i in range(per):
            joint[per * j + i] = product[:, 128 * i : 128 * (i + 1)]
        return carry

    lax.fori_loop(0, X, project, 0)

    for s in range(2):
        for g in range(pairs):
            hq[s, g : g + 1, :] = joint[g, SEG * s : SEG * s + 16, :].astype(F32)[0:1]
        for g in range(2 * pairs):
            hfl[s, g : g + 1, :] = joint[pairs + g, SEG * s : SEG * s + 16, :].astype(F32)[0:1]
    hsend[...] = hfl[...].astype(BF)

    def headers_first(c):
        own = pltpu.make_async_copy(hsend, panel.at[y, z], sems.at[0])
        own.start()
        n, f = first_axis(c)
        for t in far_first(n):
            send(hsend, panel.at[y, z], sems.at[16], sems.at[17], at_first(c, (f + t) % n))
        own.wait()

    on_core(headers_first)

    def attend(it, carry):
        p, s = it // 2, it % 2
        span = pl.ds(pl.multiple_of(s * SEG, SEG), SEG)
        queries = apart(joint[p, span, :])
        scores = lax.dot_general(queries, joint[pairs + p, span, :], NT, preferred_element_type=F32) * scale
        raised = jnp.exp(scores - jnp.max(scores, axis=-1, keepdims=True))
        shares = raised * (1.0 / jnp.sum(raised, axis=-1, keepdims=True))
        shares_buf[it] = shares
        both = jnp.dot(shares.astype(BF), joint[2 * pairs + p, span, :], preferred_element_type=F32)
        mixed[p, span, :] = joined(both).astype(BF)
        return carry

    lax.fori_loop(0, pairs, attend, 0, unroll=4)

    def hand_output_weights(c):
        if X == 4:
            for sign in (0, 1):
                settle(go.at[x, c, pl.ds(0, Y // 2)], line_recv.at[1, sign])
        send(go.at[:, c], go.at[:, c], sems.at[14], sems.at[15], partner)

    on_core(hand_output_weights)

    lax.fori_loop(pairs, 2 * pairs, attend, 0, unroll=4)


    settle_out = lambda c: settle(go.at[:, 1 - c], sems.at[15])
    on_core(settle_out)

    def mixed_all():
        return jnp.concatenate([mixed[p] for p in range(pairs)], axis=1)

    def project_out(j, carry):
        weights = jnp.concatenate([go[j, 0].reshape(D, 128), go[j, 1].reshape(D, 128)], axis=1)
        product = jnp.dot(mixed_all(), weights, preferred_element_type=F32)
        res[:, pl.ds(pl.multiple_of(j * 256, 256), 256)] = product
        return carry

    lax.fori_loop(0, X, project_out, 0)

    def headers_second(c):
        n, f = first_axis(c)
        m, s = second_axis(c)
        settle(panel.at[yz(c, pl.ds(0, n - 1), s)], sems.at[17])
        for t in far_first(m):
            ref = panel.at[yz(c, every, s)]
            send(ref, ref, sems.at[18], sems.at[19], at_second(c, (s + t) % m))

    on_core(headers_second)
    upstream_in.wait()
    for copy in small:
        copy.wait()

    block = 32
    gain_wide = gain_ref[...].astype(F32)

    def norm(i, carry):
        span = pl.ds(pl.multiple_of(i * block, block), block)
        gain = jnp.concatenate([gain_wide[p : p + 1, :] for p in range(pairs)], axis=1)
        residual = x_ref[span, :].astype(F32) + res[span, :]
        average = jnp.mean(residual, axis=-1, keepdims=True)
        centered = residual - average
        spread = jnp.mean(centered * centered, axis=-1, keepdims=True)
        inverse = lax.rsqrt(spread + 1e-05)
        normed = centered * inverse
        out_ref[span, :] = (normed * gain).astype(BF)
        scaled = u_ref[span, :].astype(F32) * gain
        first = jnp.mean(scaled, axis=-1, keepdims=True)
        second = jnp.mean(scaled * normed, axis=-1, keepdims=True)
        gradient = inverse * (scaled - first - normed * second)
        res[span, :] = gradient
        rlow[span, :] = gradient.astype(BF)
        return carry

    lax.fori_loop(0, 2 * SEG // block, norm, 0, unroll=2)
    layer_out = pltpu.make_async_copy(out_ref, out_hbm, sems.at[34])
    layer_out.start()

    for i in range(pairs):
        rlow_t[128 * i : 128 * (i + 1), :] = rlow[:, 128 * i : 128 * (i + 1)].T

    def partial_of(j, carry):
        both = jnp.concatenate([mixed[2 * j], mixed[2 * j + 1]], axis=1)
        product = jnp.dot(rlow_t[...], both, preferred_element_type=F32).astype(BF)
        part[j, 0] = product[:, :128].reshape(Y, Z, rows, 128)
        part[j, 1] = product[:, 128:].reshape(Y, Z, rows, 128)
        return carry

    def pair_send(j):
        on_core(lambda c: send(part.at[j, 1 - c], r0.at[j], sems.at[20], sems.at[21], partner))

    for j in range(X):
        partial_of(j, 0)
        if j > 0:
            pair_send(j - 1)
    pair_send(X - 1)

    tall = 2 if Y % 2 == 0 and Z * rows == 128 else 1
    height = tall * Z * rows

    def rows_of(ref, i, width):
        start = i * tall
        return jnp.concatenate(
            [
                ref[j, c, pl.ds(start, tall)].reshape(height, width)
                for j in range(X)
                for c in (0, 1)
            ],
            axis=1,
        )

    def mix_back(i, carry):
        product = lax.dot_general(rlow[...], rows_of(go, i, 128), NT, preferred_element_type=F32).astype(BF)
        for k in range(height // 128):
            mgrad[(height // 128) * i + k] = product[:, 128 * k : 128 * (k + 1)]
        return carry

    lax.fori_loop(0, Y // tall, mix_back, 0)

    settle(r0, sems.at[21])

    def pair_sum(i, carry):
        j, k = i // Y, i % Y
        a1[j, k] = (part[j, core, k].astype(F32) + r0[j, k].astype(F32)).astype(BF)
        return carry

    lax.fori_loop(0, X * Y, pair_sum, 0)

    def reduce_first(c):
        n, f = first_axis(c)
        far = (f + n // 2) % n
        kept = pltpu.make_async_copy(a1.at[(x,) + yz(c, far, every)], tie_in.at[x], sems.at[1])
        kept.start()
        for t in range(1, X):
            k = (x + t) % X
            send(a1.at[(k,) + yz(c, far, every)], tie_in.at[x], sems.at[30], sems.at[31], at_x(c, k))
        own = pltpu.make_async_copy(a1.at[(every,) + yz(c, f, every)], r1.at[0], sems.at[0])
        own.start()
        for t in far_first(n):
            if 2 * t != n:
                g = (f + t) % n
                send(a1.at[(every,) + yz(c, g, every)], r1.at[t], sems.at[22], sems.at[23], at_first(c, g))
        own.wait()
        kept.wait()

    on_core(reduce_first)

    def attend_back(it, carry):
        p, s = it // 2, it % 2
        span = pl.ds(pl.multiple_of(s * SEG, SEG), SEG)
        keys, values = joint[pairs + p, span, :], joint[2 * pairs + p, span, :]
        outer = apart(mgrad[p, span, :])
        shares = shares_buf[it]
        shares_grad = lax.dot_general(outer, values, NT, preferred_element_type=F32)
        inner = jnp.sum(shares_grad * shares, axis=-1, keepdims=True)
        scores_grad = (shares * (shares_grad - inner) * scale).astype(BF)
        query_grad = jnp.dot(scores_grad, keys, preferred_element_type=F32)
        jgrad[p, span, :] = joined(query_grad).astype(BF)
        key_grad = jnp.dot(scores_grad.T, apart(joint[p, span, :]), preferred_element_type=F32)
        jgrad[pairs + p, span, :] = key_grad.astype(BF)
        value_grad = jnp.dot(shares.astype(BF).T, outer, preferred_element_type=F32)
        jgrad[2 * pairs + p, span, :] = value_grad.astype(BF)
        return carry

    lax.fori_loop(0, pairs, attend_back, 0, unroll=4)

    if X > 1:
        settle(tie_in.at[pl.ds(0, X - 1)], sems.at[31])
    far_total = tie_in[0].astype(F32)
    for k in range(1, X):
        far_total = far_total + tie_in[k].astype(F32)
    tie_sum[...] = far_total.astype(BF)


    def far_send(c):
        n, f = first_axis(c)
        send(tie_sum, tie_got, sems.at[32], sems.at[33], at_first(c, (f + n // 2) % n))

    on_core(far_send)

    lax.fori_loop(pairs, 2 * pairs, attend_back, 0, unroll=4)

    def input_back(i, carry):
        left = jnp.concatenate([jgrad[g] for g in range(3 * pairs)], axis=1)
        product = lax.dot_general(left, rows_of(gj, i, wide), NT, preferred_element_type=F32)
        span = pl.ds(pl.multiple_of(i * height, height), height)
        grad_ref[:, span] = (res[:, span] + product).astype(BF)
        return carry

    lax.fori_loop(0, Y // tall, input_back, 0)

    gradient_out = pltpu.make_async_copy(grad_ref, grad_hbm, sems.at[35])
    gradient_out.start()

    def headers_all(c):
        m, s = second_axis(c)
        settle(panel.at[yz(c, every, pl.ds(0, m - 1))], sems.at[19])

    on_core(headers_all)

    sub = lax.broadcasted_iota(jnp.int32, (pairs, 128), 0)
    low = lax.broadcasted_iota(jnp.int32, (pairs, 128), 1) < HD
    head = 2 * sub + jnp.where(low, 0, 1)
    slopes = jnp.zeros((pairs, 128), F32)
    for h in range(2 * pairs):
        slopes = jnp.where(head == h, 2.0 ** (-(h + 1.0) * 4.0 / (2 * pairs)), slopes)
    for i in range(2):
        own_depth = depth_ref[ctx * 2 + i]
        scores, values = [], []
        for l in range(lists_ref.shape[1] + 1):
            if l == lists_ref.shape[1]:
                tile = panel[y, z, i]
                depth = own_depth
            else:
                listed = lists_ref[i, l]
                other = jnp.maximum(listed, 0)
                tile = panel[other // (2 * Z), (other // 2) % Z, other % 2]
                depth = depth_ref[other]
            product = hq[i] * tile[:pairs].astype(F32)
            score = jnp.where(
                low,
                jnp.sum(jnp.where(low, product, 0.0), axis=-1, keepdims=True),
                jnp.sum(jnp.where(low, 0.0, product), axis=-1, keepdims=True),
            )
            score = score * scale - slopes * (own_depth - depth).astype(F32)
            if l < lists_ref.shape[1]:
                score = jnp.where(listed >= 0, score, -1e30)
            scores.append(score)
            values.append(tile[pairs:].astype(F32))
        top = functools.reduce(jnp.maximum, scores)
        raised = [jnp.exp(v - top) for v in scores]
        below = 1.0 / functools.reduce(jnp.add, raised)
        context = functools.reduce(
            jnp.add, [(r * below).astype(BF).astype(F32) * v for r, v in zip(raised, values)]
        )
        for p in range(pairs):
            wide_context[i : i + 1, 128 * p : 128 * (p + 1)] = context[p : p + 1]
    context_ref[...] = wide_context[...].astype(BF)

    if Y > 2:
        settle(r1.at[pl.ds(0, Y - 2)], sems.at[23])
    settle(tie_got, sems.at[33])

    def first_sum(j, carry):
        total = r1[0, j].astype(F32)
        for k in range(1, Y):
            if 2 * k != Y:
                total = total + r1[k, j].astype(F32)
        a2[j] = total
        return carry

    lax.fori_loop(0, X, first_sum, 0)
    a2[x] = a2[x] + tie_got[...].astype(F32)
    a2_low[...] = a2[...].astype(BF)

    def reduce_second(c):
        m, s = second_axis(c)
        own = pltpu.make_async_copy(a2_low.at[:, s], r2.at[0], sems.at[0])
        own.start()
        for t in far_first(m):
            g = (s + t) % m
            send(a2_low.at[:, g], r2.at[t], sems.at[24], sems.at[25], at_second(c, g))
        own.wait()

    on_core(reduce_second)
    settle(r2.at[pl.ds(0, Y - 1)], sems.at[25])
    total = r2[0].astype(F32)
    for k in range(1, Y):
        total = total + r2[k].astype(F32)
    a3[...] = total

    own = pltpu.make_async_copy(a3.at[x], r3.at[x], sems.at[0])
    own.start()
    for t in range(1, X):
        k = (x + t) % X
        send(a3.at[k], r3.at[x], sems.at[26], sems.at[27], (k * 2 + core, ctx))
    own.wait()
    if X > 1:
        settle(r3.at[pl.ds(0, X - 1)], sems.at[27])
    final = r3[0]
    for k in range(1, X):
        final = final + r3[k]
    dw_ref[...] = final
    layer_out.wait()
    gradient_out.wait()

    def drain(c):
        n, f = first_axis(c)
        m, s = second_axis(c)
        if X > 1:
            settle(gj.at[pl.ds(0, X - 1), c, y, z], sems.at[2])
            settle(go.at[pl.ds(0, min(X - 1, 2)), c], sems.at[12])
            if X == 4:
                settle(go.at[x, c], sems.at[13])
            settle(r3.at[pl.ds(0, X - 1)], sems.at[26])
            settle(tie_in.at[pl.ds(0, X - 1)], sems.at[30])
        settle(go.at[(x, c) + yz(c, pl.ds(0, n - 1), s)], sems.at[4])
        settle(gj.at[:, c], sems.at[10])
        settle(go.at[:, c], sems.at[14])
        settle(panel.at[yz(c, pl.ds(0, n - 1), s)], sems.at[16])
        settle(r0, sems.at[20])
        if n > 2:
            settle(r1.at[pl.ds(0, n - 2)], sems.at[22])
        settle(r2.at[pl.ds(0, m - 1)], sems.at[24])
        settle(tie_sum, sems.at[32])
        settle(gj.at[(every, c) + yz(c, pl.ds(0, n - 1), s)], sems.at[6])
        settle(gj.at[(every, c) + yz(c, every, pl.ds(0, m - 1))], sems.at[7])
        settle(go.at[(x, c) + yz(c, every, pl.ds(0, m - 1))], sems.at[8])
        settle(panel.at[yz(c, every, pl.ds(0, m - 1))], sems.at[18])

    on_core(drain)


def call_layer(dims, tokens, upstream, joint_weight, output_weight, gain, lists, depth):
    X, Y, Z = dims
    T, D = tokens.shape
    pairs = D // 128
    rows, wide = joint_weight.shape
    vmem = pl.BlockSpec(memory_space=pltpu.VMEM)
    anywhere = pl.BlockSpec(memory_space=pl.ANY)
    V = pltpu.VMEM
    dma = pltpu.SemaphoreType.DMA
    most = max(Y, Z)
    return pl.pallas_call(
        functools.partial(layer_kernel, dims),
        out_shape=(
            jax.ShapeDtypeStruct((T, D), BF),
            jax.ShapeDtypeStruct((T, D), BF),
            jax.ShapeDtypeStruct((rows, 128), F32),
            jax.ShapeDtypeStruct((2, D), BF),
        ),
        in_specs=[anywhere] * 7,
        out_specs=(anywhere, anywhere, vmem, vmem),
        scratch_shapes=[
            V((T, D), BF),
            V((T, D), BF),
            V((T, D), BF),
            V((T, D), BF),
            V((Y, Z, 2, 2 * pairs, 128), BF),
            V((X, 2, Y, Z, rows, wide), BF),
            V((X, 2, Y, Z, rows, 128), BF),
            V((3 * pairs, T, 128), BF),
            V((2 * pairs, 2 * SEG, SEG), F32),
            V((pairs, T, 128), BF),
            V((T, D), F32),
            V((T, D), BF),
            V((D, T), BF),
            V((X, 2, Y, Z, rows, 128), BF),
            V((X, Y, Z, rows, 128), BF),
            V((X, Y, Z, rows, 128), BF),
            V((Y, X, Z, rows, 128), BF),
            V((X, Z, rows, 128), BF),
            V((Z, rows, 128), BF),
            V((Z, rows, 128), BF),
            V((X, Z, rows, 128), F32),
            V((X, Z, rows, 128), BF),
            V((Y, X, rows, 128), BF),
            V((X, rows, 128), F32),
            V((X, rows, 128), F32),
            V((pairs, T, 128), BF),
            V((3 * pairs, T, 128), BF),
            V((2, pairs, 128), F32),
            V((2, 2 * pairs, 128), F32),
            V((2, 2 * pairs, 128), BF),
            V((2, D), F32),
            dma((most,)),
            dma((2, most // 2, most)),
            dma((2, most // 2)),
            dma((2, 2)),
            V(gain.shape, BF),
            pltpu.SMEM(lists.shape, jnp.int32),
            pltpu.SMEM(depth.shape, jnp.int32),
            dma((39,)),
        ],
        compiler_params=pltpu.CompilerParams(collective_id=0, has_side_effects=True),
        name="segment_layer",
    )(tokens, upstream, joint_weight, output_weight, gain, lists, depth)


def on_device(
    dims, segment_tokens, upstream_grad, joint_weight, output_weight, norm_gain, ancestors, outline_depth
):
    T, D = segment_tokens.shape[1:]
    layer_output, input_gradient, weight_gradient, context = call_layer(
        dims,
        segment_tokens[0],
        upstream_grad[0],
        joint_weight,
        output_weight,
        norm_gain.reshape(D // 128, 128),
        ancestors[0],
        outline_depth[0],
    )
    return (layer_output[None], input_gradient[None], weight_gradient.T, context[None])


def solution(mesh, dims=TORUS):
    return jax.shard_map(
        functools.partial(on_device, dims),
        mesh=mesh,
        in_specs=(
            P("dp", "ctx", None),
            P("dp", "ctx", None),
            P("ctx", "dp"),
            P("ctx", "dp"),
            P(),
            P("dp", "ctx", None),
            P("dp", None),
        ),
        out_specs=(
            P("dp", "ctx", None),
            P("dp", "ctx", None),
            P("dp", "ctx"),
            P("dp", "ctx", None),
        ),
        check_vma=False,
    )
```

```python
import functools

import jax
import jax.numpy as jnp
from jax import lax
from jax.experimental import pallas as pl
from jax.experimental.pallas import tpu as pltpu
from jax.sharding import PartitionSpec as P

HD = 64
SEG = 128
BF = jnp.bfloat16
F32 = jnp.float32
MESH = pl.DeviceIdType.MESH
TORUS = (4, 8, 8)
NT = (((1,), (1,)), ((), ()))


def far_first(n):
    return sorted(range(1, n), key=lambda t: -min(t, n - t))


def layer_kernel(
    dims,
    tokens_ref,
    upstream_ref,
    wj_ref,
    wo_ref,
    gain_hbm,
    lists_hbm,
    depth_hbm,
    out_hbm,
    grad_hbm,
    dw_ref,
    context_ref,
    x_ref,
    u_ref,
    out_ref,
    grad_ref,
    panel,
    gj,
    go,
    joint,
    shares_buf,
    mixed,
    res,
    rlow,
    rlow_t,
    part,
    r0,
    a1,
    r1,
    tie_in,
    tie_sum,
    tie_got,
    a2,
    a2_low,
    r2,
    mgrad,
    jgrad,
    hq,
    hfl,
    hsend,
    wide_context,
    first_recv,
    ring_recv,
    out_recv,
    line_recv,
    gain_ref,
    lists_ref,
    depth_ref,
    sems,
):
    X, Y, Z = dims
    D = x_ref.shape[1]
    pairs = D // 128
    rows = wj_ref.shape[0]
    wide = wj_ref.shape[1]
    scale = HD ** (-0.5)
    dp = lax.axis_index("dp")
    ctx = lax.axis_index("ctx")
    x, core = dp // 2, dp % 2
    y, z = ctx // Z, ctx % Z
    every = slice(None)

    def on_core(body):
        for c in (0, 1):

            @pl.when(core == c)
            def _():
                body(c)

    def send(src, dst, ssem, rsem, peer):
        pltpu.make_async_remote_copy(
            src_ref=src, dst_ref=dst, send_sem=ssem, recv_sem=rsem, device_id=peer, device_id_type=MESH
        ).start()

    def settle(ref, sem):
        pltpu.make_async_copy(ref, ref, sem).wait()

    def first_axis(c):
        return (Y, y) if c == 0 else (Z, z)

    def second_axis(c):
        return (Z, z) if c == 0 else (Y, y)

    def at_first(c, f):
        return (dp, f * Z + z) if c == 0 else (dp, y * Z + f)

    def at_second(c, s):
        return (dp, y * Z + s) if c == 0 else (dp, s * Z + z)

    def yz(c, f, s):
        return (f, s) if c == 0 else (s, f)

    def at_x(c, k):
        return (k * 2 + c, ctx)

    partner = (x * 2 + 1 - core, ctx)

    tokens_in = pltpu.make_async_copy(tokens_ref, x_ref, sems.at[28])
    upstream_in = pltpu.make_async_copy(upstream_ref, u_ref, sems.at[29])
    tokens_in.start()
    upstream_in.start()
    small = [
        pltpu.make_async_copy(gain_hbm, gain_ref, sems.at[36]),
        pltpu.make_async_copy(lists_hbm, lists_ref, sems.at[37]),
        pltpu.make_async_copy(depth_hbm, depth_ref, sems.at[38]),
    ]
    for copy in small:
        copy.start()

    barrier = pltpu.get_barrier_semaphore()
    for t in range(1, X):
        pl.semaphore_signal(barrier, device_id=(((x + t) % X) * 2 + core, ctx), device_id_type=MESH)
    for t in range(1, Y):
        pl.semaphore_signal(barrier, device_id=(dp, ((y + t) % Y) * Z + z), device_id_type=MESH)
    for t in range(1, Z):
        pl.semaphore_signal(barrier, device_id=(dp, y * Z + (z + t) % Z), device_id_type=MESH)
    pl.semaphore_signal(barrier, device_id=partner, device_id_type=MESH)

    def greet(c):
        m, s = second_axis(c)
        for a in range(1, X):
            for t in range(1, m):
                peer = ((x + a) % X * 2 + c, at_second(c, (s + t) % m)[1])
                pl.semaphore_signal(barrier, device_id=peer, device_id_type=MESH)

    on_core(greet)
    pl.semaphore_wait(barrier, X + Y + Z - 2 + (X - 1) * (Y - 1))

    def gather(c):
        n, f = first_axis(c)
        m, s = second_axis(c)

        def block(o, q):
            return gj.at[(every, c) + yz(c, (f + o) % n, (s + q) % m)]

        def out_block(q):
            return go.at[(x, c) + yz(c, every, (s + q) % m)]

        def hop(ref, ssem, rsem, peer):
            send(ref, ref, ssem, rsem, peer)

        def step(sign):
            return 1 if sign == 0 else -1

        def on_second(sign, k, o):
            return 2 * k < m or (2 * k == m and (2 * o < n) == (sign == 0))

        def on_out(sign, k):
            return 2 * k < m or (2 * k == m and sign == 1)

        def push_second(sign, k, o):
            if on_second(sign, k, o):
                hop(
                    block(o, -step(sign) * (k - 1) % m),
                    sems.at[7],
                    ring_recv.at[sign, k - 1, o],
                    at_second(c, (s + step(sign) % m) % m),
                )

        def push_out(sign, k):
            if on_out(sign, k):
                hop(
                    out_block(-step(sign) * (k - 1) % m),
                    sems.at[8],
                    out_recv.at[sign, k - 1],
                    at_second(c, (s + step(sign) % m) % m),
                )

        def share(ref):
            hop(ref, sems.at[10], sems.at[11], partner)

        own = pltpu.make_async_copy(wj_ref, gj.at[x, c, y, z], sems.at[0])
        own_out = pltpu.make_async_copy(wo_ref, go.at[x, c, y, z], sems.at[1])
        own.start()
        own_out.start()
        for t in range(1, X):
            send(wj_ref, gj.at[x, c, y, z], sems.at[2], sems.at[3], at_x(c, (x + t) % X))
        near = sorted(range(1, n), key=lambda t: min(t, n - t))
        for t in near:
            send(wo_ref, go.at[x, c, y, z], sems.at[4], sems.at[5], at_first(c, (f + t) % n))
        own.wait()
        own_out.wait()
        if X > 1:
            settle(gj.at[pl.ds(0, X - 1), c, y, z], sems.at[3])
        for t in near:
            hop(block(0, 0), sems.at[6], first_recv.at[t], at_first(c, (f + t) % n))
        for sign in (0, 1):
            push_second(sign, 1, 0)
        share(block(0, 0))

        arrival = {-t % n: 1.5 + i for i, t in enumerate(near)}
        arrival[0] = 0.0
        events = [(arrival[o], 0, 0, "first", 0, o) for o in range(1, n)]
        for sign in (0, 1):
            for k in range(1, m // 2 + 1):
                for o in range(n):
                    if on_second(sign, k, o):
                        events.append((arrival[o] + 2.9 * k, 2, sign, "second", k, o))
                if on_out(sign, k):
                    events.append((3 + 2.9 * k, 1, sign, "out", k, 0))
        events.append((3, 1, 0, "plane", 0, 0))
        events.sort(key=lambda e: (e[0], e[1], -e[4], e[2]))
        left = sum(e[3] == "out" for e in events)
        for _, _, sign, kind, k, o in events:
            if kind == "first":
                settle(block(o, 0), first_recv.at[-o % n])
                for way in (0, 1):
                    push_second(way, 1, o)
                share(block(o, 0))
            elif kind == "second":
                ref = block(o, -step(sign) * k % m)
                settle(ref, ring_recv.at[sign, k - 1, o])
                push_second(sign, k + 1, o)
                share(ref)
            elif kind == "plane":
                settle(go.at[(x, c) + yz(c, pl.ds(0, n - 1), s)], sems.at[5])
                for way in (0, 1):
                    push_out(way, 1)
            else:
                settle(out_block(-step(sign) * k % m), out_recv.at[sign, k - 1])
                push_out(sign, k + 1)
                left -= 1
                if left == 0:
                    for sign in range(min(X - 1, 2)):
                        hop(go.at[x, c], sems.at[12], line_recv.at[0, sign], at_x(c, (x + step(sign)) % X))
        for sign in range(min(X - 1, 2)):
            settle(go.at[x, c], line_recv.at[0, sign])
            if X == 4:
                ref = go.at[(x - step(sign)) % X, c, pl.ds(sign * Y // 2, Y // 2)]
                hop(ref, sems.at[13], line_recv.at[1, sign], at_x(c, (x + step(sign)) % X))
        settle(gj.at[:, 1 - c], sems.at[11])

    on_core(gather)
    tokens_in.wait()

    lane = lax.broadcasted_iota(jnp.int32, (SEG, 128), 1)
    low_half = lane < HD

    def apart(pair):
        nothing = jnp.zeros_like(pair)
        return jnp.concatenate(
            [jnp.where(low_half, pair, nothing), jnp.where(low_half, nothing, pair)], axis=0
        )

    def joined(both):
        return jnp.where(low_half, both[:SEG], both[SEG:])

    def project(j, carry):
        weights = jnp.concatenate(
            [gj[j, 0].reshape(D, wide), gj[j, 1].reshape(D, wide)], axis=1
        )
        product = jnp.dot(x_ref[...], weights, preferred_element_type=F32).astype(BF)
        per = 2 * wide // 128
        for i in range(per):
            joint[per * j + i] = product[:, 128 * i : 128 * (i + 1)]
        return carry

    lax.fori_loop(0, X, project, 0)

    for s in range(2):
        for g in range(pairs):
            hq[s, g : g + 1, :] = joint[g, SEG * s : SEG * s + 16, :].astype(F32)[0:1]
        for g in range(2 * pairs):
            hfl[s, g : g + 1, :] = joint[pairs + g, SEG * s : SEG * s + 16, :].astype(F32)[0:1]
    hsend[...] = hfl[...].astype(BF)

    def headers_first(c):
        own = pltpu.make_async_copy(hsend, panel.at[y, z], sems.at[0])
        own.start()
        n, f = first_axis(c)
        for t in far_first(n):
            send(hsend, panel.at[y, z], sems.at[16], sems.at[17], at_first(c, (f + t) % n))
        own.wait()

    on_core(headers_first)

    def attend(it, carry):
        p, s = it // 2, it % 2
        span = pl.ds(pl.multiple_of(s * SEG, SEG), SEG)
        queries = apart(joint[p, span, :])
        scores = lax.dot_general(queries, joint[pairs + p, span, :], NT, preferred_element_type=F32) * scale
        raised = jnp.exp(scores - jnp.max(scores, axis=-1, keepdims=True))
        shares = raised * (1.0 / jnp.sum(raised, axis=-1, keepdims=True))
        shares_buf[it] = shares
        both = jnp.dot(shares.astype(BF), joint[2 * pairs + p, span, :], preferred_element_type=F32)
        mixed[p, span, :] = joined(both).astype(BF)
        return carry

    lax.fori_loop(0, pairs, attend, 0, unroll=4)

    def hand_output_weights(c):
        if X == 4:
            for sign in (0, 1):
                settle(go.at[x, c, pl.ds(0, Y // 2)], line_recv.at[1, sign])
        send(go.at[:, c], go.at[:, c], sems.at[14], sems.at[15], partner)

    on_core(hand_output_weights)

    lax.fori_loop(pairs, 2 * pairs, attend, 0, unroll=4)


    settle_out = lambda c: settle(go.at[:, 1 - c], sems.at[15])
    on_core(settle_out)

    def mixed_all():
        return jnp.concatenate([mixed[p] for p in range(pairs)], axis=1)

    def project_out(j, carry):
        weights = jnp.concatenate([go[j, 0].reshape(D, 128), go[j, 1].reshape(D, 128)], axis=1)
        product = jnp.dot(mixed_all(), weights, preferred_element_type=F32)
        res[:, pl.ds(pl.multiple_of(j * 256, 256), 256)] = product
        return carry

    lax.fori_loop(0, X, project_out, 0)

    def headers_second(c):
        n, f = first_axis(c)
        m, s = second_axis(c)
        settle(panel.at[yz(c, pl.ds(0, n - 1), s)], sems.at[17])
        for t in far_first(m):
            ref = panel.at[yz(c, every, s)]
            send(ref, ref, sems.at[18], sems.at[19], at_second(c, (s + t) % m))

    on_core(headers_second)
    upstream_in.wait()
    for copy in small:
        copy.wait()

    block = 32
    gain_wide = gain_ref[...].astype(F32)

    def norm(i, carry):
        span = pl.ds(pl.multiple_of(i * block, block), block)
        gain = jnp.concatenate([gain_wide[p : p + 1, :] for p in range(pairs)], axis=1)
        residual = x_ref[span, :].astype(F32) + res[span, :]
        average = jnp.mean(residual, axis=-1, keepdims=True)
        centered = residual - average
        spread = jnp.mean(centered * centered, axis=-1, keepdims=True)
        inverse = lax.rsqrt(spread + 1e-05)
        normed = centered * inverse
        out_ref[span, :] = (normed * gain).astype(BF)
        scaled = u_ref[span, :].astype(F32) * gain
        first = jnp.mean(scaled, axis=-1, keepdims=True)
        second = jnp.mean(scaled * normed, axis=-1, keepdims=True)
        gradient = inverse * (scaled - first - normed * second)
        res[span, :] = gradient
        rlow[span, :] = gradient.astype(BF)
        return carry

    lax.fori_loop(0, 2 * SEG // block, norm, 0, unroll=2)
    layer_out = pltpu.make_async_copy(out_ref, out_hbm, sems.at[34])
    layer_out.start()

    for i in range(pairs):
        rlow_t[128 * i : 128 * (i + 1), :] = rlow[:, 128 * i : 128 * (i + 1)].T

    def partial_of(j, carry):
        both = jnp.concatenate([mixed[2 * j], mixed[2 * j + 1]], axis=1)
        product = jnp.dot(rlow_t[...], both, preferred_element_type=F32).astype(BF)
        part[j, 0] = product[:, :128].reshape(Y, Z, rows, 128)
        part[j, 1] = product[:, 128:].reshape(Y, Z, rows, 128)
        return carry

    def pair_send(j):
        on_core(lambda c: send(part.at[j, 1 - c], r0.at[j], sems.at[20], sems.at[21], partner))

    for j in range(X):
        partial_of(j, 0)
        if j > 0:
            pair_send(j - 1)
    pair_send(X - 1)

    tall = 2 if Y % 2 == 0 and Z * rows == 128 else 1
    height = tall * Z * rows

    def rows_of(ref, i, width):
        start = i * tall
        return jnp.concatenate(
            [
                ref[j, c, pl.ds(start, tall)].reshape(height, width)
                for j in range(X)
                for c in (0, 1)
            ],
            axis=1,
        )

    def mix_back(i, carry):
        product = lax.dot_general(rlow[...], rows_of(go, i, 128), NT, preferred_element_type=F32).astype(BF)
        for k in range(height // 128):
            mgrad[(height // 128) * i + k] = product[:, 128 * k : 128 * (k + 1)]
        return carry

    lax.fori_loop(0, Y // tall, mix_back, 0)

    settle(r0, sems.at[21])

    def pair_sum(i, carry):
        j, k = i // Y, i % Y
        a1[j, k] = (part[j, core, k].astype(F32) + r0[j, k].astype(F32)).astype(BF)
        return carry

    lax.fori_loop(0, X * Y, pair_sum, 0)

    def reduce_first(c):
        n, f = first_axis(c)
        far = (f + n // 2) % n
        kept = pltpu.make_async_copy(a1.at[(x,) + yz(c, far, every)], tie_in.at[x], sems.at[1])
        kept.start()
        for t in range(1, X):
            k = (x + t) % X
            send(a1.at[(k,) + yz(c, far, every)], tie_in.at[x], sems.at[30], sems.at[31], at_x(c, k))
        own = pltpu.make_async_copy(a1.at[(every,) + yz(c, f, every)], r1.at[0], sems.at[0])
        own.start()
        for t in far_first(n):
            if 2 * t != n:
                g = (f + t) % n
                send(a1.at[(every,) + yz(c, g, every)], r1.at[t], sems.at[22], sems.at[23], at_first(c, g))
        own.wait()
        kept.wait()

    on_core(reduce_first)

    def attend_back(it, carry):
        p, s = it // 2, it % 2
        span = pl.ds(pl.multiple_of(s * SEG, SEG), SEG)
        keys, values = joint[pairs + p, span, :], joint[2 * pairs + p, span, :]
        outer = apart(mgrad[p, span, :])
        shares = shares_buf[it]
        shares_grad = lax.dot_general(outer, values, NT, preferred_element_type=F32)
        inner = jnp.sum(shares_grad * shares, axis=-1, keepdims=True)
        scores_grad = (shares * (shares_grad - inner) * scale).astype(BF)
        query_grad = jnp.dot(scores_grad, keys, preferred_element_type=F32)
        jgrad[p, span, :] = joined(query_grad).astype(BF)
        key_grad = jnp.dot(scores_grad.T, apart(joint[p, span, :]), preferred_element_type=F32)
        jgrad[pairs + p, span, :] = key_grad.astype(BF)
        value_grad = jnp.dot(shares.astype(BF).T, outer, preferred_element_type=F32)
        jgrad[2 * pairs + p, span, :] = value_grad.astype(BF)
        return carry

    lax.fori_loop(0, pairs, attend_back, 0, unroll=4)

    if X > 1:
        settle(tie_in.at[pl.ds(0, X - 1)], sems.at[31])
    far_total = tie_in[0].astype(F32)
    for k in range(1, X):
        far_total = far_total + tie_in[k].astype(F32)
    tie_sum[...] = far_total.astype(BF)


    def far_send(c):
        n, f = first_axis(c)
        send(tie_sum, tie_got, sems.at[32], sems.at[33], at_first(c, (f + n // 2) % n))

    on_core(far_send)

    lax.fori_loop(pairs, 2 * pairs, attend_back, 0, unroll=4)

    def input_back(i, carry):
        left = jnp.concatenate([jgrad[g] for g in range(3 * pairs)], axis=1)
        product = lax.dot_general(left, rows_of(gj, i, wide), NT, preferred_element_type=F32)
        span = pl.ds(pl.multiple_of(i * height, height), height)
        grad_ref[:, span] = (res[:, span] + product).astype(BF)
        return carry

    lax.fori_loop(0, Y // tall, input_back, 0)

    gradient_out = pltpu.make_async_copy(grad_ref, grad_hbm, sems.at[35])
    gradient_out.start()

    def headers_all(c):
        m, s = second_axis(c)
        settle(panel.at[yz(c, every, pl.ds(0, m - 1))], sems.at[19])

    on_core(headers_all)

    sub = lax.broadcasted_iota(jnp.int32, (pairs, 128), 0)
    low = lax.broadcasted_iota(jnp.int32, (pairs, 128), 1) < HD
    head = 2 * sub + jnp.where(low, 0, 1)
    slopes = jnp.zeros((pairs, 128), F32)
    for h in range(2 * pairs):
        slopes = jnp.where(head == h, 2.0 ** (-(h + 1.0) * 4.0 / (2 * pairs)), slopes)
    for i in range(2):
        own_depth = depth_ref[ctx * 2 + i]
        scores, values = [], []
        for l in range(lists_ref.shape[1] + 1):
            if l == lists_ref.shape[1]:
                tile = panel[y, z, i]
                depth = own_depth
            else:
                listed = lists_ref[i, l]
                other = jnp.maximum(listed, 0)
                tile = panel[other // (2 * Z), (other // 2) % Z, other % 2]
                depth = depth_ref[other]
            product = hq[i] * tile[:pairs].astype(F32)
            score = jnp.where(
                low,
                jnp.sum(jnp.where(low, product, 0.0), axis=-1, keepdims=True),
                jnp.sum(jnp.where(low, 0.0, product), axis=-1, keepdims=True),
            )
            score = score * scale - slopes * (own_depth - depth).astype(F32)
            if l < lists_ref.shape[1]:
                score = jnp.where(listed >= 0, score, -1e30)
            scores.append(score)
            values.append(tile[pairs:].astype(F32))
        top = functools.reduce(jnp.maximum, scores)
        raised = [jnp.exp(v - top) for v in scores]
        below = 1.0 / functools.reduce(jnp.add, raised)
        context = functools.reduce(
            jnp.add, [(r * below).astype(BF).astype(F32) * v for r, v in zip(raised, values)]
        )
        for p in range(pairs):
            wide_context[i : i + 1, 128 * p : 128 * (p + 1)] = context[p : p + 1]
    context_ref[...] = wide_context[...].astype(BF)

    if Y > 2:
        settle(r1.at[pl.ds(0, Y - 2)], sems.at[23])
    settle(tie_got, sems.at[33])

    def first_sum(j, carry):
        total = r1[0, j].astype(F32)
        for k in range(1, Y):
            if 2 * k != Y:
                total = total + r1[k, j].astype(F32)
        a2[j] = total
        return carry

    lax.fori_loop(0, X, first_sum, 0)
    a2[x] = a2[x] + tie_got[...].astype(F32)
    a2_low[...] = a2[...].astype(BF)

    def reduce_second(c):
        m, s = second_axis(c)
        for t in [*far_first(m), 0]:
            for a in range(X - 1, -1, -1):
                k, g = (x + a) % X, (s + t) % m
                if a == 0 and t == 0:
                    own = pltpu.make_async_copy(a2_low.at[k, g], r2.at[0], sems.at[0])
                    own.start()
                    own.wait()
                else:
                    peer = (k * 2 + c, at_second(c, g)[1])
                    send(a2_low.at[k, g], r2.at[a * m + t], sems.at[24], sems.at[25], peer)

    on_core(reduce_second)
    settle(r2.at[pl.ds(1, X * Y - 1)], sems.at[25])
    final = r2[0].astype(F32)
    for k in range(1, X * Y):
        final = final + r2[k].astype(F32)
    dw_ref[...] = final
    layer_out.wait()
    gradient_out.wait()

    def drain(c):
        n, f = first_axis(c)
        m, s = second_axis(c)
        if X > 1:
            settle(gj.at[pl.ds(0, X - 1), c, y, z], sems.at[2])
            settle(go.at[pl.ds(0, min(X - 1, 2)), c], sems.at[12])
            if X == 4:
                settle(go.at[x, c], sems.at[13])
            settle(tie_in.at[pl.ds(0, X - 1)], sems.at[30])
        settle(go.at[(x, c) + yz(c, pl.ds(0, n - 1), s)], sems.at[4])
        settle(gj.at[:, c], sems.at[10])
        settle(go.at[:, c], sems.at[14])
        settle(panel.at[yz(c, pl.ds(0, n - 1), s)], sems.at[16])
        settle(r0, sems.at[20])
        if n > 2:
            settle(r1.at[pl.ds(0, n - 2)], sems.at[22])
        settle(r2.at[pl.ds(1, X * m - 1)], sems.at[24])
        settle(tie_sum, sems.at[32])
        settle(gj.at[(every, c) + yz(c, pl.ds(0, n - 1), s)], sems.at[6])
        settle(gj.at[(every, c) + yz(c, every, pl.ds(0, m - 1))], sems.at[7])
        settle(go.at[(x, c) + yz(c, every, pl.ds(0, m - 1))], sems.at[8])
        settle(panel.at[yz(c, every, pl.ds(0, m - 1))], sems.at[18])

    on_core(drain)


def call_layer(dims, tokens, upstream, joint_weight, output_weight, gain, lists, depth):
    X, Y, Z = dims
    T, D = tokens.shape
    pairs = D // 128
    rows, wide = joint_weight.shape
    vmem = pl.BlockSpec(memory_space=pltpu.VMEM)
    anywhere = pl.BlockSpec(memory_space=pl.ANY)
    V = pltpu.VMEM
    dma = pltpu.SemaphoreType.DMA
    most = max(Y, Z)
    return pl.pallas_call(
        functools.partial(layer_kernel, dims),
        out_shape=(
            jax.ShapeDtypeStruct((T, D), BF),
            jax.ShapeDtypeStruct((T, D), BF),
            jax.ShapeDtypeStruct((rows, 128), F32),
            jax.ShapeDtypeStruct((2, D), BF),
        ),
        in_specs=[anywhere] * 7,
        out_specs=(anywhere, anywhere, vmem, vmem),
        scratch_shapes=[
            V((T, D), BF),
            V((T, D), BF),
            V((T, D), BF),
            V((T, D), BF),
            V((Y, Z, 2, 2 * pairs, 128), BF),
            V((X, 2, Y, Z, rows, wide), BF),
            V((X, 2, Y, Z, rows, 128), BF),
            V((3 * pairs, T, 128), BF),
            V((2 * pairs, 2 * SEG, SEG), F32),
            V((pairs, T, 128), BF),
            V((T, D), F32),
            V((T, D), BF),
            V((D, T), BF),
            V((X, 2, Y, Z, rows, 128), BF),
            V((X, Y, Z, rows, 128), BF),
            V((X, Y, Z, rows, 128), BF),
            V((Y, X, Z, rows, 128), BF),
            V((X, Z, rows, 128), BF),
            V((Z, rows, 128), BF),
            V((Z, rows, 128), BF),
            V((X, Z, rows, 128), F32),
            V((X, Z, rows, 128), BF),
            V((X * Y, rows, 128), BF),
            V((pairs, T, 128), BF),
            V((3 * pairs, T, 128), BF),
            V((2, pairs, 128), F32),
            V((2, 2 * pairs, 128), F32),
            V((2, 2 * pairs, 128), BF),
            V((2, D), F32),
            dma((most,)),
            dma((2, most // 2, most)),
            dma((2, most // 2)),
            dma((2, 2)),
            V(gain.shape, BF),
            pltpu.SMEM(lists.shape, jnp.int32),
            pltpu.SMEM(depth.shape, jnp.int32),
            dma((39,)),
        ],
        compiler_params=pltpu.CompilerParams(collective_id=0, has_side_effects=True),
        name="segment_layer",
    )(tokens, upstream, joint_weight, output_weight, gain, lists, depth)


def finish_kernel(*refs):
    count = len(refs) // 3
    sources, targets, held, sems = refs[:count], refs[count : 2 * count], refs[2 * count : 3 * count], refs[-1]
    arrive = [pltpu.make_async_copy(a, h, sems.at[0, i]) for i, (a, h) in enumerate(zip(sources, held))]
    leave = [pltpu.make_async_copy(h, b, sems.at[1, i]) for i, (h, b) in enumerate(zip(held, targets))]
    for copy in arrive:
        copy.start()
    for first, second in zip(arrive, leave):
        first.wait()
        second.start()
    for copy in leave:
        copy.wait()


def finish(*arrays):
    anywhere = pl.BlockSpec(memory_space=pl.ANY)
    return pl.pallas_call(
        finish_kernel,
        out_shape=tuple(jax.ShapeDtypeStruct(a.shape, a.dtype) for a in arrays),
        in_specs=[anywhere] * len(arrays),
        out_specs=(anywhere,) * len(arrays),
        scratch_shapes=[pltpu.VMEM(a.shape, a.dtype) for a in arrays]
        + [pltpu.SemaphoreType.DMA((2, len(arrays)))],
        name="hand_on",
    )(*arrays)


def on_device(
    dims, segment_tokens, upstream_grad, joint_weight, output_weight, norm_gain, ancestors, outline_depth
):
    T, D = segment_tokens.shape[1:]
    layer_output, input_gradient, weight_gradient, context = call_layer(
        dims,
        segment_tokens[0],
        upstream_grad[0],
        joint_weight,
        output_weight,
        norm_gain.reshape(D // 128, 128),
        ancestors[0],
        outline_depth[0],
    )
    layer_output, input_gradient, weight_gradient, context = finish(
        layer_output, input_gradient, weight_gradient, context
    )
    return (layer_output[None], input_gradient[None], weight_gradient.T, context[None])


def solution(mesh, dims=TORUS):
    return jax.shard_map(
        functools.partial(on_device, dims),
        mesh=mesh,
        in_specs=(
            P("dp", "ctx", None),
            P("dp", "ctx", None),
            P("ctx", "dp"),
            P("ctx", "dp"),
            P(),
            P("dp", "ctx", None),
            P("dp", None),
        ),
        out_specs=(
            P("dp", "ctx", None),
            P("dp", "ctx", None),
            P("dp", "ctx"),
            P("dp", "ctx", None),
        ),
        check_vma=False,
    )
```

```python
import functools

import jax
import jax.numpy as jnp
from jax import lax
from jax.experimental import pallas as pl
from jax.experimental.pallas import tpu as pltpu
from jax.sharding import PartitionSpec as P

HD = 64
SEG = 128
BF = jnp.bfloat16
F32 = jnp.float32
MESH = pl.DeviceIdType.MESH
TORUS = (4, 8, 8)
NT = (((1,), (1,)), ((), ()))


def far_first(n):
    return sorted(range(1, n), key=lambda t: -min(t, n - t))


def layer_kernel(
    dims,
    tokens_ref,
    upstream_ref,
    wj_ref,
    wo_ref,
    gain_hbm,
    lists_hbm,
    depth_hbm,
    out_ref,
    grad_ref,
    dw_ref,
    context_ref,
    x_ref,
    u_ref,
    panel,
    gj,
    go,
    joint,
    shares_buf,
    mixed,
    res,
    rlow,
    rlow_t,
    part,
    r0,
    a1,
    r1,
    tie_in,
    tie_sum,
    tie_got,
    a2,
    a2_low,
    r2,
    mgrad,
    jgrad,
    hq,
    hfl,
    hsend,
    wide_context,
    first_recv,
    ring_recv,
    out_recv,
    line_recv,
    gain_ref,
    lists_ref,
    depth_ref,
    sems,
):
    X, Y, Z = dims
    D = x_ref.shape[1]
    pairs = D // 128
    rows = wj_ref.shape[0]
    wide = wj_ref.shape[1]
    scale = HD ** (-0.5)
    dp = lax.axis_index("dp")
    ctx = lax.axis_index("ctx")
    x, core = dp // 2, dp % 2
    y, z = ctx // Z, ctx % Z
    every = slice(None)

    def on_core(body):
        for c in (0, 1):

            @pl.when(core == c)
            def _():
                body(c)

    def send(src, dst, ssem, rsem, peer):
        pltpu.make_async_remote_copy(
            src_ref=src, dst_ref=dst, send_sem=ssem, recv_sem=rsem, device_id=peer, device_id_type=MESH
        ).start()

    def settle(ref, sem):
        pltpu.make_async_copy(ref, ref, sem).wait()

    def first_axis(c):
        return (Y, y) if c == 0 else (Z, z)

    def second_axis(c):
        return (Z, z) if c == 0 else (Y, y)

    def at_first(c, f):
        return (dp, f * Z + z) if c == 0 else (dp, y * Z + f)

    def at_second(c, s):
        return (dp, y * Z + s) if c == 0 else (dp, s * Z + z)

    def yz(c, f, s):
        return (f, s) if c == 0 else (s, f)

    def at_x(c, k):
        return (k * 2 + c, ctx)

    partner = (x * 2 + 1 - core, ctx)

    tokens_in = pltpu.make_async_copy(tokens_ref, x_ref, sems.at[28])
    upstream_in = pltpu.make_async_copy(upstream_ref, u_ref, sems.at[29])
    tokens_in.start()
    upstream_in.start()
    small = [
        pltpu.make_async_copy(gain_hbm, gain_ref, sems.at[36]),
        pltpu.make_async_copy(lists_hbm, lists_ref, sems.at[37]),
        pltpu.make_async_copy(depth_hbm, depth_ref, sems.at[38]),
    ]
    for copy in small:
        copy.start()

    barrier = pltpu.get_barrier_semaphore()
    for t in range(1, X):
        pl.semaphore_signal(barrier, device_id=(((x + t) % X) * 2 + core, ctx), device_id_type=MESH)
    for t in range(1, Y):
        pl.semaphore_signal(barrier, device_id=(dp, ((y + t) % Y) * Z + z), device_id_type=MESH)
    for t in range(1, Z):
        pl.semaphore_signal(barrier, device_id=(dp, y * Z + (z + t) % Z), device_id_type=MESH)
    pl.semaphore_signal(barrier, device_id=partner, device_id_type=MESH)

    def greet(c):
        m, s = second_axis(c)
        for a in range(1, X):
            for t in range(1, m):
                peer = ((x + a) % X * 2 + c, at_second(c, (s + t) % m)[1])
                pl.semaphore_signal(barrier, device_id=peer, device_id_type=MESH)

    on_core(greet)
    pl.semaphore_wait(barrier, X + Y + Z - 2 + (X - 1) * (Y - 1))

    def gather(c):
        n, f = first_axis(c)
        m, s = second_axis(c)

        def block(o, q):
            return gj.at[(every, c) + yz(c, (f + o) % n, (s + q) % m)]

        def out_block(q):
            return go.at[(x, c) + yz(c, every, (s + q) % m)]

        def hop(ref, ssem, rsem, peer):
            send(ref, ref, ssem, rsem, peer)

        def step(sign):
            return 1 if sign == 0 else -1

        def on_second(sign, k, o):
            return 2 * k < m or (2 * k == m and (2 * o < n) == (sign == 0))

        def on_out(sign, k):
            return 2 * k < m or (2 * k == m and sign == 1)

        def push_second(sign, k, o):
            if on_second(sign, k, o):
                hop(
                    block(o, -step(sign) * (k - 1) % m),
                    sems.at[7],
                    ring_recv.at[sign, k - 1, o],
                    at_second(c, (s + step(sign) % m) % m),
                )

        def push_out(sign, k):
            if on_out(sign, k):
                hop(
                    out_block(-step(sign) * (k - 1) % m),
                    sems.at[8],
                    out_recv.at[sign, k - 1],
                    at_second(c, (s + step(sign) % m) % m),
                )

        def share(ref):
            hop(ref, sems.at[10], sems.at[11], partner)

        own = pltpu.make_async_copy(wj_ref, gj.at[x, c, y, z], sems.at[0])
        own_out = pltpu.make_async_copy(wo_ref, go.at[x, c, y, z], sems.at[1])
        own.start()
        own_out.start()
        for t in range(1, X):
            send(wj_ref, gj.at[x, c, y, z], sems.at[2], sems.at[3], at_x(c, (x + t) % X))
        near = sorted(range(1, n), key=lambda t: min(t, n - t))
        for t in near:
            send(wo_ref, go.at[x, c, y, z], sems.at[4], sems.at[5], at_first(c, (f + t) % n))
        own.wait()
        own_out.wait()
        if X > 1:
            settle(gj.at[pl.ds(0, X - 1), c, y, z], sems.at[3])
        for t in near:
            hop(block(0, 0), sems.at[6], first_recv.at[t], at_first(c, (f + t) % n))
        for sign in (0, 1):
            push_second(sign, 1, 0)
        share(block(0, 0))

        arrival = {-t % n: 1.5 + i for i, t in enumerate(near)}
        arrival[0] = 0.0
        events = [(arrival[o], 0, 0, "first", 0, o) for o in range(1, n)]
        for sign in (0, 1):
            for k in range(1, m // 2 + 1):
                for o in range(n):
                    if on_second(sign, k, o):
                        events.append((arrival[o] + 2.9 * k, 2, sign, "second", k, o))
                if on_out(sign, k):
                    events.append((3 + 2.9 * k, 1, sign, "out", k, 0))
        events.append((3, 1, 0, "plane", 0, 0))
        events.sort(key=lambda e: (e[0], e[1], -e[4], e[2]))
        left = sum(e[3] == "out" for e in events)
        for _, _, sign, kind, k, o in events:
            if kind == "first":
                settle(block(o, 0), first_recv.at[-o % n])
                for way in (0, 1):
                    push_second(way, 1, o)
                share(block(o, 0))
            elif kind == "second":
                ref = block(o, -step(sign) * k % m)
                settle(ref, ring_recv.at[sign, k - 1, o])
                push_second(sign, k + 1, o)
                share(ref)
            elif kind == "plane":
                settle(go.at[(x, c) + yz(c, pl.ds(0, n - 1), s)], sems.at[5])
                for way in (0, 1):
                    push_out(way, 1)
            else:
                settle(out_block(-step(sign) * k % m), out_recv.at[sign, k - 1])
                push_out(sign, k + 1)
                left -= 1
                if left == 0:
                    for sign in range(min(X - 1, 2)):
                        hop(go.at[x, c], sems.at[12], line_recv.at[0, sign], at_x(c, (x + step(sign)) % X))
        for sign in range(min(X - 1, 2)):
            settle(go.at[x, c], line_recv.at[0, sign])
            if X == 4:
                ref = go.at[(x - step(sign)) % X, c, pl.ds(sign * Y // 2, Y // 2)]
                hop(ref, sems.at[13], line_recv.at[1, sign], at_x(c, (x + step(sign)) % X))
        settle(gj.at[:, 1 - c], sems.at[11])

    on_core(gather)
    tokens_in.wait()

    lane = lax.broadcasted_iota(jnp.int32, (SEG, 128), 1)
    low_half = lane < HD

    def apart(pair):
        nothing = jnp.zeros_like(pair)
        return jnp.concatenate(
            [jnp.where(low_half, pair, nothing), jnp.where(low_half, nothing, pair)], axis=0
        )

    def joined(both):
        return jnp.where(low_half, both[:SEG], both[SEG:])

    def project(j, carry):
        weights = jnp.concatenate(
            [gj[j, 0].reshape(D, wide), gj[j, 1].reshape(D, wide)], axis=1
        )
        product = jnp.dot(x_ref[...], weights, preferred_element_type=F32).astype(BF)
        per = 2 * wide // 128
        for i in range(per):
            joint[per * j + i] = product[:, 128 * i : 128 * (i + 1)]
        return carry

    lax.fori_loop(0, X, project, 0)

    for s in range(2):
        for g in range(pairs):
            hq[s, g : g + 1, :] = joint[g, SEG * s : SEG * s + 16, :].astype(F32)[0:1]
        for g in range(2 * pairs):
            hfl[s, g : g + 1, :] = joint[pairs + g, SEG * s : SEG * s + 16, :].astype(F32)[0:1]
    hsend[...] = hfl[...].astype(BF)

    def headers_first(c):
        own = pltpu.make_async_copy(hsend, panel.at[y, z], sems.at[0])
        own.start()
        n, f = first_axis(c)
        for t in far_first(n):
            send(hsend, panel.at[y, z], sems.at[16], sems.at[17], at_first(c, (f + t) % n))
        own.wait()

    on_core(headers_first)

    def attend(it, carry):
        p, s = it // 2, it % 2
        span = pl.ds(pl.multiple_of(s * SEG, SEG), SEG)
        queries = apart(joint[p, span, :])
        scores = lax.dot_general(queries, joint[pairs + p, span, :], NT, preferred_element_type=F32) * scale
        raised = jnp.exp(scores - jnp.max(scores, axis=-1, keepdims=True))
        shares = raised * (1.0 / jnp.sum(raised, axis=-1, keepdims=True))
        shares_buf[it] = shares
        both = jnp.dot(shares.astype(BF), joint[2 * pairs + p, span, :], preferred_element_type=F32)
        mixed[p, span, :] = joined(both).astype(BF)
        return carry

    lax.fori_loop(0, pairs, attend, 0, unroll=8)

    def hand_output_weights(c):
        if X == 4:
            for sign in (0, 1):
                settle(go.at[x, c, pl.ds(0, Y // 2)], line_recv.at[1, sign])
        send(go.at[:, c], go.at[:, c], sems.at[14], sems.at[15], partner)

    on_core(hand_output_weights)

    lax.fori_loop(pairs, 2 * pairs, attend, 0, unroll=8)


    settle_out = lambda c: settle(go.at[:, 1 - c], sems.at[15])
    on_core(settle_out)

    def mixed_all():
        return jnp.concatenate([mixed[p] for p in range(pairs)], axis=1)

    def project_out(j, carry):
        weights = jnp.concatenate([go[j, 0].reshape(D, 128), go[j, 1].reshape(D, 128)], axis=1)
        product = jnp.dot(mixed_all(), weights, preferred_element_type=F32)
        res[:, pl.ds(pl.multiple_of(j * 256, 256), 256)] = product
        return carry

    lax.fori_loop(0, X, project_out, 0)

    def headers_second(c):
        n, f = first_axis(c)
        m, s = second_axis(c)
        settle(panel.at[yz(c, pl.ds(0, n - 1), s)], sems.at[17])
        for t in far_first(m):
            ref = panel.at[yz(c, every, s)]
            send(ref, ref, sems.at[18], sems.at[19], at_second(c, (s + t) % m))

    on_core(headers_second)
    upstream_in.wait()
    for copy in small:
        copy.wait()

    block = 32
    gain_wide = gain_ref[...].astype(F32)

    def norm(i, carry):
        span = pl.ds(pl.multiple_of(i * block, block), block)
        gain = jnp.concatenate([gain_wide[p : p + 1, :] for p in range(pairs)], axis=1)
        residual = x_ref[span, :].astype(F32) + res[span, :]
        average = jnp.mean(residual, axis=-1, keepdims=True)
        centered = residual - average
        spread = jnp.mean(centered * centered, axis=-1, keepdims=True)
        inverse = lax.rsqrt(spread + 1e-05)
        normed = centered * inverse
        out_ref[span, :] = (normed * gain).astype(BF)
        scaled = u_ref[span, :].astype(F32) * gain
        first = jnp.mean(scaled, axis=-1, keepdims=True)
        second = jnp.mean(scaled * normed, axis=-1, keepdims=True)
        gradient = inverse * (scaled - first - normed * second)
        res[span, :] = gradient
        rlow[span, :] = gradient.astype(BF)
        return carry

    lax.fori_loop(0, 2 * SEG // block, norm, 0, unroll=4)

    for i in range(pairs):
        rlow_t[128 * i : 128 * (i + 1), :] = rlow[:, 128 * i : 128 * (i + 1)].T

    def partial_of(j, carry):
        both = jnp.concatenate([mixed[2 * j], mixed[2 * j + 1]], axis=1)
        product = jnp.dot(rlow_t[...], both, preferred_element_type=F32).astype(BF)
        part[j, 0] = product[:, :128].reshape(Y, Z, rows, 128)
        part[j, 1] = product[:, 128:].reshape(Y, Z, rows, 128)
        return carry

    def pair_send(j):
        on_core(lambda c: send(part.at[j, 1 - c], r0.at[j], sems.at[20], sems.at[21], partner))

    for j in range(X):
        partial_of(j, 0)
        if j > 0:
            pair_send(j - 1)
    pair_send(X - 1)

    tall = 2 if Y % 2 == 0 and Z * rows == 128 else 1
    height = tall * Z * rows

    def rows_of(ref, i, width):
        start = i * tall
        return jnp.concatenate(
            [
                ref[j, c, pl.ds(start, tall)].reshape(height, width)
                for j in range(X)
                for c in (0, 1)
            ],
            axis=1,
        )

    def mix_back(i, carry):
        product = lax.dot_general(rlow[...], rows_of(go, i, 128), NT, preferred_element_type=F32).astype(BF)
        for k in range(height // 128):
            mgrad[(height // 128) * i + k] = product[:, 128 * k : 128 * (k + 1)]
        return carry

    lax.fori_loop(0, Y // tall, mix_back, 0)

    settle(r0, sems.at[21])

    def pair_sum(i, carry):
        j, k = i // Y, i % Y
        a1[j, k] = (part[j, core, k].astype(F32) + r0[j, k].astype(F32)).astype(BF)
        return carry

    lax.fori_loop(0, X * Y, pair_sum, 0)

    def reduce_first(c):
        n, f = first_axis(c)
        far = (f + n // 2) % n
        kept = pltpu.make_async_copy(a1.at[(x,) + yz(c, far, every)], tie_in.at[x], sems.at[1])
        kept.start()
        for t in range(1, X):
            k = (x + t) % X
            send(a1.at[(k,) + yz(c, far, every)], tie_in.at[x], sems.at[30], sems.at[31], at_x(c, k))
        own = pltpu.make_async_copy(a1.at[(every,) + yz(c, f, every)], r1.at[0], sems.at[0])
        own.start()
        for t in far_first(n):
            if 2 * t != n:
                g = (f + t) % n
                send(a1.at[(every,) + yz(c, g, every)], r1.at[t], sems.at[22], sems.at[23], at_first(c, g))
        own.wait()
        kept.wait()

    on_core(reduce_first)

    def attend_back(it, carry):
        p, s = it // 2, it % 2
        span = pl.ds(pl.multiple_of(s * SEG, SEG), SEG)
        keys, values = joint[pairs + p, span, :], joint[2 * pairs + p, span, :]
        outer = apart(mgrad[p, span, :])
        shares = shares_buf[it]
        shares_grad = lax.dot_general(outer, values, NT, preferred_element_type=F32)
        inner = jnp.sum(shares_grad * shares, axis=-1, keepdims=True)
        scores_grad = (shares * (shares_grad - inner) * scale).astype(BF)
        query_grad = jnp.dot(scores_grad, keys, preferred_element_type=F32)
        jgrad[p, span, :] = joined(query_grad).astype(BF)
        key_grad = jnp.dot(scores_grad.T, apart(joint[p, span, :]), preferred_element_type=F32)
        jgrad[pairs + p, span, :] = key_grad.astype(BF)
        value_grad = jnp.dot(shares.astype(BF).T, outer, preferred_element_type=F32)
        jgrad[2 * pairs + p, span, :] = value_grad.astype(BF)
        return carry

    lax.fori_loop(0, pairs, attend_back, 0, unroll=8)

    if X > 1:
        settle(tie_in.at[pl.ds(0, X - 1)], sems.at[31])
    far_total = tie_in[0].astype(F32)
    for k in range(1, X):
        far_total = far_total + tie_in[k].astype(F32)
    tie_sum[...] = far_total.astype(BF)


    def far_send(c):
        n, f = first_axis(c)
        send(tie_sum, tie_got, sems.at[32], sems.at[33], at_first(c, (f + n // 2) % n))

    on_core(far_send)

    lax.fori_loop(pairs, 2 * pairs, attend_back, 0, unroll=8)

    def input_back(i, carry):
        left = jnp.concatenate([jgrad[g] for g in range(3 * pairs)], axis=1)
        product = lax.dot_general(left, rows_of(gj, i, wide), NT, preferred_element_type=F32)
        span = pl.ds(pl.multiple_of(i * height, height), height)
        grad_ref[:, span] = (res[:, span] + product).astype(BF)
        return carry

    lax.fori_loop(0, Y // tall, input_back, 0)


    def headers_all(c):
        m, s = second_axis(c)
        settle(panel.at[yz(c, every, pl.ds(0, m - 1))], sems.at[19])

    on_core(headers_all)

    sub = lax.broadcasted_iota(jnp.int32, (pairs, 128), 0)
    low = lax.broadcasted_iota(jnp.int32, (pairs, 128), 1) < HD
    head = 2 * sub + jnp.where(low, 0, 1)
    slopes = jnp.zeros((pairs, 128), F32)
    for h in range(2 * pairs):
        slopes = jnp.where(head == h, 2.0 ** (-(h + 1.0) * 4.0 / (2 * pairs)), slopes)
    for i in range(2):
        own_depth = depth_ref[ctx * 2 + i]
        scores, values = [], []
        for l in range(lists_ref.shape[1] + 1):
            if l == lists_ref.shape[1]:
                tile = panel[y, z, i]
                depth = own_depth
            else:
                listed = lists_ref[i, l]
                other = jnp.maximum(listed, 0)
                tile = panel[other // (2 * Z), (other // 2) % Z, other % 2]
                depth = depth_ref[other]
            product = hq[i] * tile[:pairs].astype(F32)
            score = jnp.where(
                low,
                jnp.sum(jnp.where(low, product, 0.0), axis=-1, keepdims=True),
                jnp.sum(jnp.where(low, 0.0, product), axis=-1, keepdims=True),
            )
            score = score * scale - slopes * (own_depth - depth).astype(F32)
            if l < lists_ref.shape[1]:
                score = jnp.where(listed >= 0, score, -1e30)
            scores.append(score)
            values.append(tile[pairs:].astype(F32))
        top = functools.reduce(jnp.maximum, scores)
        raised = [jnp.exp(v - top) for v in scores]
        below = 1.0 / functools.reduce(jnp.add, raised)
        context = functools.reduce(
            jnp.add, [(r * below).astype(BF).astype(F32) * v for r, v in zip(raised, values)]
        )
        for p in range(pairs):
            wide_context[i : i + 1, 128 * p : 128 * (p + 1)] = context[p : p + 1]
    context_ref[...] = wide_context[...].astype(BF)

    if Y > 2:
        settle(r1.at[pl.ds(0, Y - 2)], sems.at[23])
    settle(tie_got, sems.at[33])

    def first_sum(j, carry):
        total = r1[0, j].astype(F32)
        for k in range(1, Y):
            if 2 * k != Y:
                total = total + r1[k, j].astype(F32)
        a2[j] = total
        return carry

    lax.fori_loop(0, X, first_sum, 0)
    a2[x] = a2[x] + tie_got[...].astype(F32)
    a2_low[...] = a2[...].astype(BF)

    def reduce_second(c):
        m, s = second_axis(c)
        for t in [*far_first(m), 0]:
            for a in range(X - 1, -1, -1):
                k, g = (x + a) % X, (s + t) % m
                if a == 0 and t == 0:
                    own = pltpu.make_async_copy(a2_low.at[k, g], r2.at[0], sems.at[0])
                    own.start()
                    own.wait()
                else:
                    peer = (k * 2 + c, at_second(c, g)[1])
                    send(a2_low.at[k, g], r2.at[a * m + t], sems.at[24], sems.at[25], peer)

    on_core(reduce_second)
    settle(r2.at[pl.ds(1, X * Y - 1)], sems.at[25])
    final = r2[0].astype(F32)
    for k in range(1, X * Y):
        final = final + r2[k].astype(F32)
    dw_ref[...] = final

    def drain(c):
        n, f = first_axis(c)
        m, s = second_axis(c)
        if X > 1:
            settle(gj.at[pl.ds(0, X - 1), c, y, z], sems.at[2])
            settle(go.at[pl.ds(0, min(X - 1, 2)), c], sems.at[12])
            if X == 4:
                settle(go.at[x, c], sems.at[13])
            settle(tie_in.at[pl.ds(0, X - 1)], sems.at[30])
        settle(go.at[(x, c) + yz(c, pl.ds(0, n - 1), s)], sems.at[4])
        settle(gj.at[:, c], sems.at[10])
        settle(go.at[:, c], sems.at[14])
        settle(panel.at[yz(c, pl.ds(0, n - 1), s)], sems.at[16])
        settle(r0, sems.at[20])
        if n > 2:
            settle(r1.at[pl.ds(0, n - 2)], sems.at[22])
        settle(r2.at[pl.ds(1, X * m - 1)], sems.at[24])
        settle(tie_sum, sems.at[32])
        settle(gj.at[(every, c) + yz(c, pl.ds(0, n - 1), s)], sems.at[6])
        settle(gj.at[(every, c) + yz(c, every, pl.ds(0, m - 1))], sems.at[7])
        settle(go.at[(x, c) + yz(c, every, pl.ds(0, m - 1))], sems.at[8])
        settle(panel.at[yz(c, every, pl.ds(0, m - 1))], sems.at[18])

    on_core(drain)


def call_layer(dims, tokens, upstream, joint_weight, output_weight, gain, lists, depth):
    X, Y, Z = dims
    T, D = tokens.shape
    pairs = D // 128
    rows, wide = joint_weight.shape
    vmem = pl.BlockSpec(memory_space=pltpu.VMEM)
    anywhere = pl.BlockSpec(memory_space=pl.ANY)
    V = pltpu.VMEM
    dma = pltpu.SemaphoreType.DMA
    most = max(Y, Z)
    return pl.pallas_call(
        functools.partial(layer_kernel, dims),
        out_shape=(
            V((T, D), BF),
            V((T, D), BF),
            V((rows, 128), F32),
            V((2, D), BF),
        ),
        in_specs=[anywhere] * 7,
        out_specs=(vmem,) * 4,
        scratch_shapes=[
            V((T, D), BF),
            V((T, D), BF),
            V((Y, Z, 2, 2 * pairs, 128), BF),
            V((X, 2, Y, Z, rows, wide), BF),
            V((X, 2, Y, Z, rows, 128), BF),
            V((3 * pairs, T, 128), BF),
            V((2 * pairs, 2 * SEG, SEG), F32),
            V((pairs, T, 128), BF),
            V((T, D), F32),
            V((T, D), BF),
            V((D, T), BF),
            V((X, 2, Y, Z, rows, 128), BF),
            V((X, Y, Z, rows, 128), BF),
            V((X, Y, Z, rows, 128), BF),
            V((Y, X, Z, rows, 128), BF),
            V((X, Z, rows, 128), BF),
            V((Z, rows, 128), BF),
            V((Z, rows, 128), BF),
            V((X, Z, rows, 128), F32),
            V((X, Z, rows, 128), BF),
            V((X * Y, rows, 128), BF),
            V((pairs, T, 128), BF),
            V((3 * pairs, T, 128), BF),
            V((2, pairs, 128), F32),
            V((2, 2 * pairs, 128), F32),
            V((2, 2 * pairs, 128), BF),
            V((2, D), F32),
            dma((most,)),
            dma((2, most // 2, most)),
            dma((2, most // 2)),
            dma((2, 2)),
            V(gain.shape, BF),
            pltpu.SMEM(lists.shape, jnp.int32),
            pltpu.SMEM(depth.shape, jnp.int32),
            dma((39,)),
        ],
        compiler_params=pltpu.CompilerParams(collective_id=0, has_side_effects=True),
        name="segment_layer",
    )(tokens, upstream, joint_weight, output_weight, gain, lists, depth)


def finish_kernel(*refs):
    count = len(refs) // 2
    copies = [
        pltpu.make_async_copy(a, b, refs[-1].at[i])
        for i, (a, b) in enumerate(zip(refs[:count], refs[count : 2 * count]))
    ]
    for copy in copies:
        copy.start()
    for copy in copies:
        copy.wait()


def finish(*arrays):
    anywhere = pl.BlockSpec(memory_space=pl.ANY)
    return pl.pallas_call(
        finish_kernel,
        out_shape=tuple(jax.ShapeDtypeStruct(a.shape, a.dtype) for a in arrays),
        in_specs=[anywhere] * len(arrays),
        out_specs=(anywhere,) * len(arrays),
        compiler_params=pltpu.CompilerParams(vmem_limit_bytes=1 << 20),
        scratch_shapes=[pltpu.SemaphoreType.DMA((len(arrays),))],
        name="hand_on",
    )(*arrays)


def on_device(
    dims, segment_tokens, upstream_grad, joint_weight, output_weight, norm_gain, ancestors, outline_depth
):
    T, D = segment_tokens.shape[1:]
    layer_output, input_gradient, weight_gradient, context = call_layer(
        dims,
        segment_tokens[0],
        upstream_grad[0],
        joint_weight,
        output_weight,
        norm_gain.reshape(D // 128, 128),
        ancestors[0],
        outline_depth[0],
    )
    layer_output, input_gradient, weight_gradient, context = finish(
        layer_output, input_gradient, weight_gradient, context
    )
    return (layer_output[None], input_gradient[None], weight_gradient.T, context[None])


def solution(mesh, dims=TORUS):
    return jax.shard_map(
        functools.partial(on_device, dims),
        mesh=mesh,
        in_specs=(
            P("dp", "ctx", None),
            P("dp", "ctx", None),
            P("ctx", "dp"),
            P("ctx", "dp"),
            P(),
            P("dp", "ctx", None),
            P("dp", None),
        ),
        out_specs=(
            P("dp", "ctx", None),
            P("dp", "ctx", None),
            P("dp", "ctx"),
            P("dp", "ctx", None),
        ),
        check_vma=False,
    )
```

```python
import functools

import jax
import jax.numpy as jnp
from jax import lax
from jax.experimental import pallas as pl
from jax.experimental.pallas import tpu as pltpu
from jax.sharding import PartitionSpec as P

HD = 64
SEG = 128
BF = jnp.bfloat16
F32 = jnp.float32
MESH = pl.DeviceIdType.MESH
TORUS = (4, 8, 8)
NT = (((1,), (1,)), ((), ()))


def far_first(n):
    return sorted(range(1, n), key=lambda t: -min(t, n - t))


def layer_kernel(
    dims,
    tokens_ref,
    upstream_ref,
    wj_ref,
    wo_ref,
    gain_hbm,
    lists_hbm,
    depth_hbm,
    out_ref,
    grad_ref,
    dw_ref,
    context_ref,
    x_ref,
    u_ref,
    panel,
    gj,
    go,
    joint,
    shares_buf,
    mixed,
    res,
    rlow,
    rlow_t,
    part,
    r0,
    a1,
    r1,
    tie_in,
    tie_sum,
    tie_got,
    a2,
    a2_low,
    r2,
    mgrad,
    jgrad,
    hq,
    hfl,
    hsend,
    wide_context,
    first_recv,
    ring_recv,
    out_recv,
    line_recv,
    gain_ref,
    lists_ref,
    depth_ref,
    sems,
):
    X, Y, Z = dims
    D = x_ref.shape[1]
    pairs = D // 128
    rows = wj_ref.shape[0]
    wide = wj_ref.shape[1]
    scale = HD ** (-0.5)
    dp = lax.axis_index("dp")
    ctx = lax.axis_index("ctx")
    x, core = dp // 2, dp % 2
    y, z = ctx // Z, ctx % Z
    every = slice(None)

    def on_core(body):
        for c in (0, 1):

            @pl.when(core == c)
            def _():
                body(c)

    def send(src, dst, ssem, rsem, peer):
        pltpu.make_async_remote_copy(
            src_ref=src, dst_ref=dst, send_sem=ssem, recv_sem=rsem, device_id=peer, device_id_type=MESH
        ).start()

    def settle(ref, sem):
        pltpu.make_async_copy(ref, ref, sem).wait()

    def first_axis(c):
        return (Y, y) if c == 0 else (Z, z)

    def second_axis(c):
        return (Z, z) if c == 0 else (Y, y)

    def at_first(c, f):
        return (dp, f * Z + z) if c == 0 else (dp, y * Z + f)

    def at_second(c, s):
        return (dp, y * Z + s) if c == 0 else (dp, s * Z + z)

    def yz(c, f, s):
        return (f, s) if c == 0 else (s, f)

    def at_x(c, k):
        return (k * 2 + c, ctx)

    partner = (x * 2 + 1 - core, ctx)

    tokens_in = pltpu.make_async_copy(tokens_ref, x_ref, sems.at[28])
    upstream_in = pltpu.make_async_copy(upstream_ref, u_ref, sems.at[29])
    tokens_in.start()
    upstream_in.start()
    small = [
        pltpu.make_async_copy(gain_hbm, gain_ref, sems.at[36]),
        pltpu.make_async_copy(lists_hbm, lists_ref, sems.at[37]),
        pltpu.make_async_copy(depth_hbm, depth_ref, sems.at[38]),
    ]
    for copy in small:
        copy.start()

    barrier = pltpu.get_barrier_semaphore()
    for t in range(1, X):
        pl.semaphore_signal(barrier, device_id=(((x + t) % X) * 2 + core, ctx), device_id_type=MESH)
    for t in range(1, Y):
        pl.semaphore_signal(barrier, device_id=(dp, ((y + t) % Y) * Z + z), device_id_type=MESH)
    for t in range(1, Z):
        pl.semaphore_signal(barrier, device_id=(dp, y * Z + (z + t) % Z), device_id_type=MESH)
    pl.semaphore_signal(barrier, device_id=partner, device_id_type=MESH)

    def greet(c):
        m, s = second_axis(c)
        for a in range(1, X):
            for t in range(1, m):
                peer = ((x + a) % X * 2 + c, at_second(c, (s + t) % m)[1])
                pl.semaphore_signal(barrier, device_id=peer, device_id_type=MESH)

    on_core(greet)
    pl.semaphore_wait(barrier, X + Y + Z - 2 + (X - 1) * (Y - 1))

    def gather(c):
        n, f = first_axis(c)
        m, s = second_axis(c)

        def block(o, q):
            return gj.at[(every, c) + yz(c, (f + o) % n, (s + q) % m)]

        def out_block(q):
            return go.at[(x, c) + yz(c, every, (s + q) % m)]

        def hop(ref, ssem, rsem, peer):
            send(ref, ref, ssem, rsem, peer)

        def step(sign):
            return 1 if sign == 0 else -1

        def on_second(sign, k, o):
            return 2 * k < m or (2 * k == m and (2 * o < n) == (sign == 0))

        def on_out(sign, k):
            return 2 * k < m or (2 * k == m and sign == 1)

        def push_second(sign, k, o):
            if on_second(sign, k, o):
                hop(
                    block(o, -step(sign) * (k - 1) % m),
                    sems.at[7],
                    ring_recv.at[sign, k - 1, o],
                    at_second(c, (s + step(sign) % m) % m),
                )

        def push_out(sign, k):
            if on_out(sign, k):
                hop(
                    out_block(-step(sign) * (k - 1) % m),
                    sems.at[8],
                    out_recv.at[sign, k - 1],
                    at_second(c, (s + step(sign) % m) % m),
                )

        def share(ref):
            hop(ref, sems.at[10], sems.at[11], partner)

        own = pltpu.make_async_copy(wj_ref, gj.at[x, c, y, z], sems.at[0])
        own_out = pltpu.make_async_copy(wo_ref, go.at[x, c, y, z], sems.at[1])
        own.start()
        own_out.start()
        for t in range(1, X):
            send(wj_ref, gj.at[x, c, y, z], sems.at[2], sems.at[3], at_x(c, (x + t) % X))
        near = sorted(range(1, n), key=lambda t: min(t, n - t))
        for t in near:
            send(wo_ref, go.at[x, c, y, z], sems.at[4], sems.at[5], at_first(c, (f + t) % n))
        own.wait()
        own_out.wait()
        if X > 1:
            settle(gj.at[pl.ds(0, X - 1), c, y, z], sems.at[3])
        for t in near:
            hop(block(0, 0), sems.at[6], first_recv.at[t], at_first(c, (f + t) % n))
        for sign in (0, 1):
            push_second(sign, 1, 0)
        share(block(0, 0))

        arrival = {-t % n: 1.5 + i for i, t in enumerate(near)}
        arrival[0] = 0.0
        events = [(arrival[o], 0, 0, "first", 0, o) for o in range(1, n)]
        for sign in (0, 1):
            for k in range(1, m // 2 + 1):
                for o in range(n):
                    if on_second(sign, k, o):
                        events.append((arrival[o] + 2.9 * k, 2, sign, "second", k, o))
                if on_out(sign, k):
                    events.append((3 + 2.9 * k, 1, sign, "out", k, 0))
        events.append((3, 1, 0, "plane", 0, 0))
        events.sort(key=lambda e: (e[0], e[1], -e[4], e[2]))
        left = sum(e[3] == "out" for e in events)
        for _, _, sign, kind, k, o in events:
            if kind == "first":
                settle(block(o, 0), first_recv.at[-o % n])
                for way in (0, 1):
                    push_second(way, 1, o)
                share(block(o, 0))
            elif kind == "second":
                ref = block(o, -step(sign) * k % m)
                settle(ref, ring_recv.at[sign, k - 1, o])
                push_second(sign, k + 1, o)
                share(ref)
            elif kind == "plane":
                settle(go.at[(x, c) + yz(c, pl.ds(0, n - 1), s)], sems.at[5])
                for way in (0, 1):
                    push_out(way, 1)
            else:
                settle(out_block(-step(sign) * k % m), out_recv.at[sign, k - 1])
                push_out(sign, k + 1)
                left -= 1
                if left == 0:
                    for sign in range(min(X - 1, 2)):
                        hop(go.at[x, c], sems.at[12], line_recv.at[0, sign], at_x(c, (x + step(sign)) % X))
        for sign in range(min(X - 1, 2)):
            settle(go.at[x, c], line_recv.at[0, sign])
            if X == 4:
                ref = go.at[(x - step(sign)) % X, c, pl.ds(sign * Y // 2, Y // 2)]
                hop(ref, sems.at[13], line_recv.at[1, sign], at_x(c, (x + step(sign)) % X))
        settle(gj.at[:, 1 - c], sems.at[11])

    on_core(gather)
    tokens_in.wait()

    lane = lax.broadcasted_iota(jnp.int32, (SEG, 128), 1)
    low_half = lane < HD

    def apart(pair):
        nothing = jnp.zeros_like(pair)
        return jnp.concatenate(
            [jnp.where(low_half, pair, nothing), jnp.where(low_half, nothing, pair)], axis=0
        )

    def joined(both):
        return jnp.where(low_half, both[:SEG], both[SEG:])

    def project(j, carry):
        weights = jnp.concatenate(
            [gj[j, 0].reshape(D, wide), gj[j, 1].reshape(D, wide)], axis=1
        )
        product = jnp.dot(x_ref[...], weights, preferred_element_type=F32).astype(BF)
        per = 2 * wide // 128
        for i in range(per):
            joint[per * j + i] = product[:, 128 * i : 128 * (i + 1)]
        return carry

    lax.fori_loop(0, X, project, 0)

    for s in range(2):
        for g in range(pairs):
            hq[s, g : g + 1, :] = joint[g, SEG * s : SEG * s + 16, :].astype(F32)[0:1]
        for g in range(2 * pairs):
            hfl[s, g : g + 1, :] = joint[pairs + g, SEG * s : SEG * s + 16, :].astype(F32)[0:1]
    hsend[...] = hfl[...].astype(BF)

    def headers_first(c):
        own = pltpu.make_async_copy(hsend, panel.at[y, z], sems.at[0])
        own.start()
        n, f = first_axis(c)
        for t in far_first(n):
            send(hsend, panel.at[y, z], sems.at[16], sems.at[17], at_first(c, (f + t) % n))
        own.wait()

    on_core(headers_first)

    def attend(it, carry):
        p, s = it // 2, it % 2
        span = pl.ds(pl.multiple_of(s * SEG, SEG), SEG)
        queries = apart(joint[p, span, :])
        scores = lax.dot_general(queries, joint[pairs + p, span, :], NT, preferred_element_type=F32) * scale
        raised = jnp.exp(scores - jnp.max(scores, axis=-1, keepdims=True))
        shares = raised * (1.0 / jnp.sum(raised, axis=-1, keepdims=True))
        shares_buf[it] = shares
        both = jnp.dot(shares.astype(BF), joint[2 * pairs + p, span, :], preferred_element_type=F32)
        mixed[p, span, :] = joined(both).astype(BF)
        return carry

    lax.fori_loop(0, pairs, attend, 0, unroll=8)

    def hand_output_weights(c):
        if X == 4:
            for sign in (0, 1):
                settle(go.at[x, c, pl.ds(0, Y // 2)], line_recv.at[1, sign])
        send(go.at[:, c], go.at[:, c], sems.at[14], sems.at[15], partner)

    on_core(hand_output_weights)

    lax.fori_loop(pairs, 2 * pairs, attend, 0, unroll=8)


    settle_out = lambda c: settle(go.at[:, 1 - c], sems.at[15])
    on_core(settle_out)

    def mixed_all():
        return jnp.concatenate([mixed[p] for p in range(pairs)], axis=1)

    def project_out(j, carry):
        weights = jnp.concatenate([go[j, 0].reshape(D, 128), go[j, 1].reshape(D, 128)], axis=1)
        product = jnp.dot(mixed_all(), weights, preferred_element_type=F32)
        res[:, pl.ds(pl.multiple_of(j * 256, 256), 256)] = product
        return carry

    lax.fori_loop(0, X, project_out, 0)

    def headers_second(c):
        n, f = first_axis(c)
        m, s = second_axis(c)
        settle(panel.at[yz(c, pl.ds(0, n - 1), s)], sems.at[17])
        for t in far_first(m):
            ref = panel.at[yz(c, every, s)]
            send(ref, ref, sems.at[18], sems.at[19], at_second(c, (s + t) % m))

    on_core(headers_second)
    upstream_in.wait()
    for copy in small:
        copy.wait()

    block = 32
    gain_wide = gain_ref[...].astype(F32)

    def norm(i, carry):
        span = pl.ds(pl.multiple_of(i * block, block), block)
        gain = jnp.concatenate([gain_wide[p : p + 1, :] for p in range(pairs)], axis=1)
        residual = x_ref[span, :].astype(F32) + res[span, :]
        average = jnp.mean(residual, axis=-1, keepdims=True)
        centered = residual - average
        spread = jnp.mean(centered * centered, axis=-1, keepdims=True)
        inverse = lax.rsqrt(spread + 1e-05)
        normed = centered * inverse
        out_ref[span, :] = (normed * gain).astype(BF)
        scaled = u_ref[span, :].astype(F32) * gain
        first = jnp.mean(scaled, axis=-1, keepdims=True)
        second = jnp.mean(scaled * normed, axis=-1, keepdims=True)
        gradient = inverse * (scaled - first - normed * second)
        res[span, :] = gradient
        rlow[span, :] = gradient.astype(BF)
        return carry

    lax.fori_loop(0, 2 * SEG // block, norm, 0, unroll=4)

    for i in range(pairs):
        rlow_t[128 * i : 128 * (i + 1), :] = rlow[:, 128 * i : 128 * (i + 1)].T

    def partial_of(j, carry):
        both = jnp.concatenate([mixed[2 * j], mixed[2 * j + 1]], axis=1)
        product = jnp.dot(rlow_t[...], both, preferred_element_type=F32).astype(BF)
        part[j, 0] = product[:, :128].reshape(Y, Z, rows, 128)
        part[j, 1] = product[:, 128:].reshape(Y, Z, rows, 128)
        return carry

    def pair_send(j):
        on_core(lambda c: send(part.at[j, 1 - c], r0.at[j], sems.at[20], sems.at[21 if 2 * j < X else 26], partner))

    for j in range(X):
        partial_of(j, 0)
        if j > 0:
            pair_send(j - 1)
    pair_send(X - 1)

    tall = 2 if Y % 2 == 0 and Z * rows == 128 else 1
    height = tall * Z * rows

    def rows_of(ref, i, width):
        start = i * tall
        return jnp.concatenate(
            [
                ref[j, c, pl.ds(start, tall)].reshape(height, width)
                for j in range(X)
                for c in (0, 1)
            ],
            axis=1,
        )

    def mix_back(i, carry):
        product = lax.dot_general(rlow[...], rows_of(go, i, 128), NT, preferred_element_type=F32).astype(BF)
        for k in range(height // 128):
            mgrad[(height // 128) * i + k] = product[:, 128 * k : 128 * (k + 1)]
        return carry

    lax.fori_loop(0, Y // tall, mix_back, 0)

    def pair_sum(i, carry):
        j, k = i // Y, i % Y
        a1[j, k] = (part[j, core, k].astype(F32) + r0[j, k].astype(F32)).astype(BF)
        return carry

    halves = [(0, X)] if X == 1 else [(0, X // 2), (X // 2, X)]

    def near_send(first, last):
        def body(c):
            n, f = first_axis(c)
            for t in far_first(n):
                if 2 * t != n:
                    g = (f + t) % n
                    span = pl.ds(first, last - first)
                    send(
                        a1.at[(span,) + yz(c, g, every)],
                        r1.at[t, span],
                        sems.at[22],
                        sems.at[23],
                        at_first(c, g),
                    )

        on_core(body)

    for which, (first, last) in enumerate(halves):
        settle(r0.at[pl.ds(first, last - first)], sems.at[(21, 26)[which]])
        lax.fori_loop(first * Y, last * Y, pair_sum, 0)
        if which + 1 < len(halves):
            near_send(first, last)

    def reduce_first(c):
        n, f = first_axis(c)
        far = (f + n // 2) % n
        kept = pltpu.make_async_copy(a1.at[(x,) + yz(c, far, every)], tie_in.at[x], sems.at[1])
        kept.start()
        for t in range(1, X):
            k = (x + t) % X
            send(a1.at[(k,) + yz(c, far, every)], tie_in.at[x], sems.at[30], sems.at[31], at_x(c, k))
        own = pltpu.make_async_copy(a1.at[(every,) + yz(c, f, every)], r1.at[0], sems.at[0])
        own.start()
        own.wait()
        kept.wait()

    on_core(reduce_first)
    near_send(*halves[-1])

    def attend_back(it, carry):
        p, s = it // 2, it % 2
        span = pl.ds(pl.multiple_of(s * SEG, SEG), SEG)
        keys, values = joint[pairs + p, span, :], joint[2 * pairs + p, span, :]
        outer = apart(mgrad[p, span, :])
        shares = shares_buf[it]
        shares_grad = lax.dot_general(outer, values, NT, preferred_element_type=F32)
        inner = jnp.sum(shares_grad * shares, axis=-1, keepdims=True)
        scores_grad = (shares * (shares_grad - inner) * scale).astype(BF)
        query_grad = jnp.dot(scores_grad, keys, preferred_element_type=F32)
        jgrad[p, span, :] = joined(query_grad).astype(BF)
        key_grad = jnp.dot(scores_grad.T, apart(joint[p, span, :]), preferred_element_type=F32)
        jgrad[pairs + p, span, :] = key_grad.astype(BF)
        value_grad = jnp.dot(shares.astype(BF).T, outer, preferred_element_type=F32)
        jgrad[2 * pairs + p, span, :] = value_grad.astype(BF)
        return carry

    lax.fori_loop(0, pairs, attend_back, 0, unroll=8)

    if X > 1:
        settle(tie_in.at[pl.ds(0, X - 1)], sems.at[31])
    far_total = tie_in[0].astype(F32)
    for k in range(1, X):
        far_total = far_total + tie_in[k].astype(F32)
    tie_sum[...] = far_total.astype(BF)


    def far_send(c):
        n, f = first_axis(c)
        send(tie_sum, tie_got, sems.at[32], sems.at[33], at_first(c, (f + n // 2) % n))

    on_core(far_send)

    lax.fori_loop(pairs, 2 * pairs, attend_back, 0, unroll=8)

    def input_back(i, carry):
        left = jnp.concatenate([jgrad[g] for g in range(3 * pairs)], axis=1)
        product = lax.dot_general(left, rows_of(gj, i, wide), NT, preferred_element_type=F32)
        span = pl.ds(pl.multiple_of(i * height, height), height)
        grad_ref[:, span] = (res[:, span] + product).astype(BF)
        return carry

    lax.fori_loop(0, Y // tall, input_back, 0)


    def headers_all(c):
        m, s = second_axis(c)
        settle(panel.at[yz(c, every, pl.ds(0, m - 1))], sems.at[19])

    on_core(headers_all)

    sub = lax.broadcasted_iota(jnp.int32, (pairs, 128), 0)
    low = lax.broadcasted_iota(jnp.int32, (pairs, 128), 1) < HD
    head = 2 * sub + jnp.where(low, 0, 1)
    slopes = jnp.zeros((pairs, 128), F32)
    for h in range(2 * pairs):
        slopes = jnp.where(head == h, 2.0 ** (-(h + 1.0) * 4.0 / (2 * pairs)), slopes)
    for i in range(2):
        own_depth = depth_ref[ctx * 2 + i]
        scores, values = [], []
        for l in range(lists_ref.shape[1] + 1):
            if l == lists_ref.shape[1]:
                tile = panel[y, z, i]
                depth = own_depth
            else:
                listed = lists_ref[i, l]
                other = jnp.maximum(listed, 0)
                tile = panel[other // (2 * Z), (other // 2) % Z, other % 2]
                depth = depth_ref[other]
            product = hq[i] * tile[:pairs].astype(F32)
            score = jnp.where(
                low,
                jnp.sum(jnp.where(low, product, 0.0), axis=-1, keepdims=True),
                jnp.sum(jnp.where(low, 0.0, product), axis=-1, keepdims=True),
            )
            score = score * scale - slopes * (own_depth - depth).astype(F32)
            if l < lists_ref.shape[1]:
                score = jnp.where(listed >= 0, score, -1e30)
            scores.append(score)
            values.append(tile[pairs:].astype(F32))
        top = functools.reduce(jnp.maximum, scores)
        raised = [jnp.exp(v - top) for v in scores]
        below = 1.0 / functools.reduce(jnp.add, raised)
        context = functools.reduce(
            jnp.add, [(r * below).astype(BF).astype(F32) * v for r, v in zip(raised, values)]
        )
        for p in range(pairs):
            wide_context[i : i + 1, 128 * p : 128 * (p + 1)] = context[p : p + 1]
    context_ref[...] = wide_context[...].astype(BF)

    if Y > 2:
        settle(r1.at[pl.ds(0, Y - 2)], sems.at[23])
    settle(tie_got, sems.at[33])

    def first_sum(j, carry):
        total = r1[0, j].astype(F32)
        for k in range(1, Y):
            if 2 * k != Y:
                total = total + r1[k, j].astype(F32)
        a2[j] = total
        return carry

    lax.fori_loop(0, X, first_sum, 0)
    a2[x] = a2[x] + tie_got[...].astype(F32)
    a2_low[...] = a2[...].astype(BF)

    def reduce_second(c):
        m, s = second_axis(c)
        for t in [*far_first(m), 0]:
            for a in range(X - 1, -1, -1):
                k, g = (x + a) % X, (s + t) % m
                if a == 0 and t == 0:
                    own = pltpu.make_async_copy(a2_low.at[k, g], r2.at[0], sems.at[0])
                    own.start()
                    own.wait()
                else:
                    peer = (k * 2 + c, at_second(c, g)[1])
                    send(a2_low.at[k, g], r2.at[a * m + t], sems.at[24], sems.at[25], peer)

    on_core(reduce_second)
    settle(r2.at[pl.ds(1, X * Y - 1)], sems.at[25])
    final = r2[0].astype(F32)
    for k in range(1, X * Y):
        final = final + r2[k].astype(F32)
    dw_ref[...] = final

    def drain(c):
        n, f = first_axis(c)
        m, s = second_axis(c)
        if X > 1:
            settle(gj.at[pl.ds(0, X - 1), c, y, z], sems.at[2])
            settle(go.at[pl.ds(0, min(X - 1, 2)), c], sems.at[12])
            if X == 4:
                settle(go.at[x, c], sems.at[13])
            settle(tie_in.at[pl.ds(0, X - 1)], sems.at[30])
        settle(go.at[(x, c) + yz(c, pl.ds(0, n - 1), s)], sems.at[4])
        settle(gj.at[:, c], sems.at[10])
        settle(go.at[:, c], sems.at[14])
        settle(panel.at[yz(c, pl.ds(0, n - 1), s)], sems.at[16])
        settle(r0, sems.at[20])
        if n > 2:
            settle(r1.at[pl.ds(0, n - 2)], sems.at[22])
        settle(r2.at[pl.ds(1, X * m - 1)], sems.at[24])
        settle(tie_sum, sems.at[32])
        settle(gj.at[(every, c) + yz(c, pl.ds(0, n - 1), s)], sems.at[6])
        settle(gj.at[(every, c) + yz(c, every, pl.ds(0, m - 1))], sems.at[7])
        settle(go.at[(x, c) + yz(c, every, pl.ds(0, m - 1))], sems.at[8])
        settle(panel.at[yz(c, every, pl.ds(0, m - 1))], sems.at[18])

    on_core(drain)


def call_layer(dims, tokens, upstream, joint_weight, output_weight, gain, lists, depth):
    X, Y, Z = dims
    T, D = tokens.shape
    pairs = D // 128
    rows, wide = joint_weight.shape
    vmem = pl.BlockSpec(memory_space=pltpu.VMEM)
    anywhere = pl.BlockSpec(memory_space=pl.ANY)
    V = pltpu.VMEM
    dma = pltpu.SemaphoreType.DMA
    most = max(Y, Z)
    return pl.pallas_call(
        functools.partial(layer_kernel, dims),
        out_shape=(
            V((T, D), BF),
            V((T, D), BF),
            V((rows, 128), F32),
            V((2, D), BF),
        ),
        in_specs=[anywhere] * 7,
        out_specs=(vmem,) * 4,
        scratch_shapes=[
            V((T, D), BF),
            V((T, D), BF),
            V((Y, Z, 2, 2 * pairs, 128), BF),
            V((X, 2, Y, Z, rows, wide), BF),
            V((X, 2, Y, Z, rows, 128), BF),
            V((3 * pairs, T, 128), BF),
            V((2 * pairs, 2 * SEG, SEG), F32),
            V((pairs, T, 128), BF),
            V((T, D), F32),
            V((T, D), BF),
            V((D, T), BF),
            V((X, 2, Y, Z, rows, 128), BF),
            V((X, Y, Z, rows, 128), BF),
            V((X, Y, Z, rows, 128), BF),
            V((Y, X, Z, rows, 128), BF),
            V((X, Z, rows, 128), BF),
            V((Z, rows, 128), BF),
            V((Z, rows, 128), BF),
            V((X, Z, rows, 128), F32),
            V((X, Z, rows, 128), BF),
            V((X * Y, rows, 128), BF),
            V((pairs, T, 128), BF),
            V((3 * pairs, T, 128), BF),
            V((2, pairs, 128), F32),
            V((2, 2 * pairs, 128), F32),
            V((2, 2 * pairs, 128), BF),
            V((2, D), F32),
            dma((most,)),
            dma((2, most // 2, most)),
            dma((2, most // 2)),
            dma((2, 2)),
            V(gain.shape, BF),
            pltpu.SMEM(lists.shape, jnp.int32),
            pltpu.SMEM(depth.shape, jnp.int32),
            dma((39,)),
        ],
        compiler_params=pltpu.CompilerParams(collective_id=0, has_side_effects=True),
        name="segment_layer",
    )(tokens, upstream, joint_weight, output_weight, gain, lists, depth)


def finish_kernel(*refs):
    count = len(refs) // 2
    copies = [
        pltpu.make_async_copy(a, b, refs[-1].at[i])
        for i, (a, b) in enumerate(zip(refs[:count], refs[count : 2 * count]))
    ]
    for copy in copies:
        copy.start()
    for copy in copies:
        copy.wait()


def finish(*arrays):
    anywhere = pl.BlockSpec(memory_space=pl.ANY)
    return pl.pallas_call(
        finish_kernel,
        out_shape=tuple(jax.ShapeDtypeStruct(a.shape, a.dtype) for a in arrays),
        in_specs=[anywhere] * len(arrays),
        out_specs=(anywhere,) * len(arrays),
        compiler_params=pltpu.CompilerParams(vmem_limit_bytes=1 << 20),
        scratch_shapes=[pltpu.SemaphoreType.DMA((len(arrays),))],
        name="hand_on",
    )(*arrays)


def on_device(
    dims, segment_tokens, upstream_grad, joint_weight, output_weight, norm_gain, ancestors, outline_depth
):
    T, D = segment_tokens.shape[1:]
    layer_output, input_gradient, weight_gradient, context = call_layer(
        dims,
        segment_tokens[0],
        upstream_grad[0],
        joint_weight,
        output_weight,
        norm_gain.reshape(D // 128, 128),
        ancestors[0],
        outline_depth[0],
    )
    layer_output, input_gradient, weight_gradient, context = finish(
        layer_output, input_gradient, weight_gradient, context
    )
    return (layer_output[None], input_gradient[None], weight_gradient.T, context[None])


def solution(mesh, dims=TORUS):
    return jax.shard_map(
        functools.partial(on_device, dims),
        mesh=mesh,
        in_specs=(
            P("dp", "ctx", None),
            P("dp", "ctx", None),
            P("ctx", "dp"),
            P("ctx", "dp"),
            P(),
            P("dp", "ctx", None),
            P("dp", None),
        ),
        out_specs=(
            P("dp", "ctx", None),
            P("dp", "ctx", None),
            P("dp", "ctx"),
            P("dp", "ctx", None),
        ),
        check_vma=False,
    )
```
